32 devices in a mesh: grp: 2 (over core), tile: 16 (over z, y, x).
Axes of the slice: x: 2, y: 2, z: 4, core: 2. Of those that a mesh axis runs over, the one named last changes fastest.
Arguments:
- right_side: float32 [64, 8192], P('grp', 'tile'), may hold values from -8 to 8
- diagonal: float32 [64, 8192], P('grp', 'tile'), may hold values from 0.25 to 2
- inverse_factor: float32 [2048, 2048], P(('grp', 'tile')), may hold values from -2 to 2, as said below
Outputs:
- solution_field: float32 [64, 8192], P('grp', 'tile')
The draws below stay inside these ranges and needn't reach their ends.
Inputs may be any that keep to these rules, and one draw needn't show every extreme that they name: `inverse_factor`: zero above the diagonal; the diagonal lies between 1 and 2.
All inputs are finite; a program needn't handle non-finite values.
Results may differ from the reference program's by a relative error of at most 0.0003.
Values sent between devices are 32-bit elements; how exact they have to be, the bound alone decides.
No kernel may reach another device: no remote copies, remote signals or barrier semaphores. Data moves between devices by JAX's collectives and lax.ppermute only.
A program may use at most 64 MiB of HBM per device.

```python
import jax
import jax.numpy as jnp
from jax import lax

RD = 32
CD = 512
FAC = 16
SWEEPS = 4
CYCLES = 2
NCO = 2048
NR = 64
NC = 8192
N_GRP = 2
N_TILE = 16


def draw_inverse_factor(key, part):
    key_diag = jax.random.fold_in(key, 11)
    key_off = jax.random.fold_in(key, 23)
    diag_vals = jax.random.uniform(key_diag, (NCO,), jnp.float32, 1.0, 2.0)
    off = jax.random.normal(key_off, (NCO, NCO), jnp.float32) * (0.4 / jnp.sqrt(NCO * 1.0))
    off = jnp.clip(jnp.tril(off, -1), -0.9, 0.9)
    return off + jnp.diag(diag_vals)


def block_scale(stream_key, dims, pieces, low, top_value):
    loudness, own = 1.0, jax.random.fold_in(stream_key, 6)
    for position, parts in pieces:
        draws = jnp.exp(jax.random.uniform(jax.random.fold_in(own, position), (parts,), jnp.float32, low / len(pieces), top_value / len(pieces)))
        loudness = loudness * jnp.repeat(draws, dims[position] // parts).reshape([-1 if axis == position else 1 for axis in range(len(dims))])
    return loudness


def scatter_about(key, dims, scale, reach, shards=(), kind=jnp.bfloat16):
    result = scale * jax.random.normal(key, dims, jnp.float32)
    if shards:
        result = result * block_scale(key, dims, shards, -0.22, 0.18)
    return jnp.clip(result, -reach, reach).astype(kind)


def setup_inputs(seed: int = 0) -> dict:
    keys = jax.random.split(jax.random.key(seed), 4)
    right_side = scatter_about(keys[0], (NR, NC), 1.0, 8.0, ((0, 2), (1, 16)), jnp.float32)
    diagonal = jnp.clip(0.25 + 1.75 * jax.random.uniform(keys[1], (NR, NC), jnp.float32) ** block_scale(keys[1], (NR, NC), ((0, 2), (1, 16)), -0.2, 0.2), 0.25, 2.0)
    inverse_factor = draw_inverse_factor(jax.random.fold_in(keys[3], 71), 0)
    return dict(right_side=right_side, diagonal=diagonal, inverse_factor=inverse_factor)


def operate(field, diagonal):
    padded = jnp.pad(field, 1)
    beside = padded[2:, 1:-1] + padded[:-2, 1:-1] + padded[1:-1, 2:] + padded[1:-1, :-2]
    beside = beside + padded[2:, :-2] + padded[:-2, 2:]
    return (6.0 + diagonal) * field - beside


def restrict(field):
    blocks = field.reshape(N_GRP, RD // FAC, FAC, N_TILE, CD // FAC, FAC)
    means = jnp.mean(blocks, axis=(2, 5))
    return jnp.transpose(means, (0, 2, 1, 3)).reshape(-1)


def prolong(values):
    blocks = values.reshape(N_GRP, N_TILE, RD // FAC, CD // FAC)
    blocks = jnp.transpose(blocks, (0, 2, 1, 3))
    blocks = jnp.repeat(jnp.repeat(blocks, FAC, axis=1), FAC, axis=3)
    return blocks.reshape(N_GRP * RD, N_TILE * CD)


def reference(right_side, diagonal, inverse_factor):
    scale = 1.0 / (6.0 + diagonal)
    solution_field = jnp.zeros_like(right_side)
    for cycle in range(CYCLES):
        residual = right_side - operate(solution_field, diagonal)
        smoothed = 0.8 * residual * scale
        for sweep in range(SWEEPS - 1):
            smoothed = smoothed + 0.8 * (residual - operate(smoothed, diagonal)) * scale
        coarse_rhs = restrict(residual)
        inner = jnp.dot(inverse_factor, coarse_rhs, precision=lax.Precision.HIGHEST)
        coarse_fix = jnp.dot(inner, inverse_factor, precision=lax.Precision.HIGHEST)
        solution_field = solution_field + smoothed + 0.5 * prolong(coarse_fix)
    return solution_field
```

```python
import functools

import jax
import jax.numpy as jnp
from jax import lax
from jax.experimental import pallas as pl
from jax.experimental.pallas import tpu as pltpu
from jax.sharding import PartitionSpec as P

FAC = 16
SWEEPS = 4
OMEGA = 0.8
MIX = 0.5
LANES = 128
SUB = 8
HALO = 8

VMEM = pl.BlockSpec(memory_space=pltpu.VMEM)


def call(body, shapes, count, scratch=()):
    return pl.pallas_call(
        body,
        out_shape=[jax.ShapeDtypeStruct(s, jnp.float32) for s in shapes],
        in_specs=[VMEM] * count,
        out_specs=[VMEM] * len(shapes),
        scratch_shapes=[pltpu.VMEM(s, jnp.float32) for s in scratch],
    )


def lane_iota(shape):
    return lax.broadcasted_iota(jnp.int32, shape, len(shape) - 1)


def row_iota(shape):
    return lax.broadcasted_iota(jnp.int32, shape, 0)


def shift(x, by, axis):
    return pltpu.roll(x, by % x.shape[axis], axis)


def neighbour_sum(x):
    above, below = shift(x, 1, 0), shift(x, -1, 0)
    return above + below + shift(x + above, -1, 1) + shift(x + below, 1, 1)


def gather_lanes(x, index):
    return jnp.take_along_axis(x, index, axis=1)


def pack_lanes(strip, first):
    step = LANES // HALO
    parts = []
    for at in range(0, strip.shape[0], step):
        piece = strip[at : at + step]
        lane, row = lane_iota(piece.shape), row_iota(piece.shape)
        piece = gather_lanes(piece, first + lax.rem(lane, HALO))
        piece = jnp.where(lane // HALO == row, piece, 0.0)
        parts.append(jnp.sum(piece, axis=0, keepdims=True))
    return parts


def start_kernel(grid, rhs_ref, diag_ref, slots_ref, edge_a_ref, edge_b_ref):
    groups, tiles = grid
    g, t = lax.axis_index("grp"), lax.axis_index("tile")
    rows, cols = rhs_ref.shape
    count = groups * tiles
    per_row = cols // FAC
    even = lax.rem(g, 2) == 0
    for at, ref in ((0, rhs_ref), (HALO, diag_ref)):
        first, last = ref[:HALO, :], ref[rows - HALO :, :]
        edge_a_ref[at : at + HALO, :] = jnp.where(even, last, first)
        if groups > 2:
            edge_b_ref[at : at + HALO, :] = jnp.where(even, first, last)
    sums = []
    for ref in (rhs_ref, diag_ref):
        for a in range(rows // FAC):
            sums.append(jnp.sum(ref[a * FAC : (a + 1) * FAC, :], axis=0, keepdims=True))
    tall = jnp.concatenate(sums + [jnp.zeros((SUB - len(sums), cols), jnp.float32)], axis=0)
    pick = (
        lax.broadcasted_iota(jnp.int32, (cols, LANES), 0) // FAC
        == lax.rem(lane_iota((cols, LANES)), per_row)
    ).astype(jnp.float32)
    means = jnp.dot(
        tall, pick, precision=lax.Precision.HIGHEST, preferred_element_type=jnp.float32
    ) * (1.0 / (FAC * FAC))
    group_of = lane_iota((1, LANES)) // per_row
    coarse = jnp.zeros((1, LANES), jnp.float32)
    for k in range(LANES // per_row):
        coarse = jnp.where(group_of == k, means[k : k + 1, :], coarse)
    to_left = lax.rem(row_iota((count, LANES)), tiles) < t
    at = 0
    for ref in (rhs_ref, diag_ref):
        left = pack_lanes(ref[:, :LANES], 0)
        right = pack_lanes(ref[:, cols - LANES :], LANES - HALO)
        for one, two in zip(left, right):
            slots_ref[:, at : at + LANES] = jnp.where(
                to_left,
                jnp.broadcast_to(one, (count, LANES)),
                jnp.broadcast_to(two, (count, LANES)),
            )
            at += LANES
    slots_ref[:, at : at + LANES] = jnp.broadcast_to(coarse, (count, LANES))


def two_products(vector, factor_ref):
    high = factor_ref.shape[1] // LANES
    total = None
    for m in range(high):
        term = factor_ref[:, m * LANES : (m + 1) * LANES] * vector[m : m + 1, :]
        total = term if total is None else total + term
    inner = jnp.sum(total, axis=1, keepdims=True)
    return [
        jnp.sum(factor_ref[:, m * LANES : (m + 1) * LANES] * inner, axis=0, keepdims=True)
        for m in range(high)
    ]


def interleave(even, odd):
    return jnp.where(lane_iota(even.shape) < LANES // 2, even, odd)


def pairs(ref, at, line_ref):
    count = ref.shape[0]
    line_ref[...] = ref[:, at : at + LANES]
    return (
        line_ref[pl.ds(0, count // 2, stride=2), :],
        line_ref[pl.ds(1, count // 2, stride=2), :],
    )


def first_kernel(got_ref, factor_ref, keep_ref, send_ref, mean_ref, line_ref):
    high = factor_ref.shape[1] // LANES
    even, odd = pairs(got_ref, got_ref.shape[1] - LANES, line_ref)
    half = LANES // 2
    mean_ref[...] = interleave(shift(even, half, 1), odd)
    terms = two_products(interleave(even, shift(odd, half, 1)), factor_ref)
    own = lax.rem(lax.axis_index("grp"), 2) == 0
    for m in range(high // 2):
        low, top = terms[m], terms[m + high // 2]
        keep_ref[m : m + 1, :] = jnp.where(own, low, top)
        send_ref[m : m + 1, :] = jnp.where(own, top, low)


def inside_mask(grid, rows, cols):
    groups, tiles = grid
    g, t = lax.axis_index("grp"), lax.axis_index("tile")
    shape = (rows + 2 * HALO, cols + LANES)
    row, lane = row_iota(shape), lane_iota(shape)
    row_ok = (row < rows) | ((row < rows + HALO) & (g < groups - 1)) | ((row >= rows + HALO) & (g > 0))
    lane_ok = (
        (lane < cols)
        | ((lane < cols + HALO) & (t < tiles - 1))
        | ((lane >= cols + LANES - HALO) & (t > 0))
    )
    return row_ok & lane_ok


def unpack_lanes(lines_ref, device, at, rows):
    step = LANES // HALO
    shape = (step, LANES)
    index = row_iota(shape) * HALO + lax.rem(lane_iota(shape), HALO)
    parts = []
    for k in range(rows // step):
        line = lines_ref[at + k, pl.ds(device, 1), :]
        parts.append(gather_lanes(jnp.broadcast_to(line, shape), index))
    return jnp.concatenate(parts, axis=0)


def smooth_kernel(
    grid, got_ref, rhs_ref, diag_ref, below_ref, above_ref,
    rhs_out, diag_out, weight_out, smooth_out, coarse_out, lines_ref,
):
    groups, tiles = grid
    g, t = lax.axis_index("grp"), lax.axis_index("tile")
    rows, cols = rhs_ref.shape
    up, down = jnp.maximum(g - 1, 0), jnp.minimum(g + 1, groups - 1)
    left, right = jnp.maximum(t - 1, 0), jnp.minimum(t + 1, tiles - 1)
    inside = inside_mask(grid, rows, cols)
    for k in range(lines_ref.shape[0]):
        lines_ref[k] = got_ref[:, k * LANES : (k + 1) * LANES]
    at = 0
    for ref, out, edge in ((rhs_ref, rhs_out, 0), (diag_ref, diag_out, HALO)):
        out[:rows, :cols] = ref[...]
        out[rows : rows + HALO, :cols] = below_ref[edge : edge + HALO, :]
        out[rows + HALO :, :cols] = above_ref[edge : edge + HALO, :]
        sides = []
        for column in (right, left):
            mid = unpack_lanes(lines_ref, g * tiles + column, at, rows)
            low = unpack_lanes(lines_ref, down * tiles + column, at, rows)[:HALO]
            top = unpack_lanes(lines_ref, up * tiles + column, at, rows)[rows - HALO :]
            sides.append(jnp.concatenate([mid, low, top], axis=0))
        lane = lane_iota(sides[0].shape)
        side = jnp.where(lane < HALO, sides[0], 0.0)
        side = jnp.where(lane >= LANES - HALO, sides[1], side)
        out[:, cols:] = side
        at += rows * HALO // LANES
    rhs = jnp.where(inside, rhs_out[...], 0.0)
    diag = jnp.where(inside, diag_out[...], 0.0)
    rhs_out[...] = rhs
    diag_out[...] = diag
    weight = jnp.where(inside, OMEGA / (6.0 + diag), 0.0)
    weight_out[...] = weight
    smooth = weight * rhs
    for _ in range(SWEEPS - 1):
        smooth = (1.0 - OMEGA) * smooth + weight * (rhs + neighbour_sum(smooth))
    smooth_out[...] = smooth
    left_over = (rhs - (6.0 + diag) * smooth + neighbour_sum(smooth))[:rows, :cols]
    per_row = cols // FAC
    sums = [
        jnp.sum(left_over[a * FAC : (a + 1) * FAC], axis=0, keepdims=True)
        for a in range(rows // FAC)
    ]
    tall = jnp.concatenate(sums + [jnp.zeros((SUB - len(sums), cols), jnp.float32)], axis=0)
    pick = (
        lax.broadcasted_iota(jnp.int32, (cols, LANES), 0) // FAC
        == lax.rem(lane_iota((cols, LANES)), per_row)
    ).astype(jnp.float32)
    means = jnp.dot(
        tall, pick, precision=lax.Precision.HIGHEST, preferred_element_type=jnp.float32
    ) * (1.0 / (FAC * FAC))
    group_of = lax.rem(lane_iota((1, LANES)) // per_row, rows // FAC)
    coarse = jnp.zeros((1, LANES), jnp.float32)
    for a in range(rows // FAC):
        coarse = jnp.where(group_of == a, means[a : a + 1, :], coarse)
    coarse_out[...] = jnp.broadcast_to(coarse, (SUB, LANES))


def spread_kernel(keep_ref, came_ref, coarse_ref, slots_ref):
    count = slots_ref.shape[0]
    high = keep_ref.shape[0]
    half = keep_ref[...] + came_ref[...]
    for m in range(high):
        slots_ref[:, m * LANES : (m + 1) * LANES] = jnp.broadcast_to(
            half[m : m + 1, :], (count, LANES)
        )
    slots_ref[:, high * LANES :] = jnp.broadcast_to(coarse_ref[:1, :], (count, LANES))


def coarse_operator(value, mean, grid, blocks):
    groups, tiles = grid
    block_rows, per_row = blocks
    here = block_rows * per_row
    shape = value.shape
    lane, row = lane_iota(shape), row_iota(shape)
    device = row * (LANES // here) + lane // here
    a = lax.rem(lane, here) // per_row
    b = lax.rem(lane, per_row)
    tile, group = lax.rem(device, tiles), device // tiles
    per_line = tiles * here // LANES

    def to_right(x):
        near = shift(x, 1, 1)
        far = shift(x, here - per_row + 1, 1)
        far = jnp.where(lane < here, shift(far, 1, 0), far)
        return jnp.where(b > 0, near, jnp.where(tile > 0, far, 0.0))

    def to_left(x):
        near = shift(x, -1, 1)
        far = shift(x, -(here - per_row + 1), 1)
        far = jnp.where(lane >= LANES - here, shift(far, -1, 0), far)
        return jnp.where(b < per_row - 1, near, jnp.where(tile < tiles - 1, far, 0.0))

    def to_below(x):
        near = shift(x, per_row, 1)
        far = shift(shift(x, -(here - per_row), 1), per_line, 0)
        return jnp.where(a > 0, near, jnp.where(group > 0, far, 0.0))

    def to_above(x):
        near = shift(x, -per_row, 1)
        far = shift(shift(x, here - per_row, 1), -per_line, 0)
        return jnp.where(a < block_rows - 1, near, jnp.where(group < groups - 1, far, 0.0))

    above, below = to_below(value), to_above(value)
    sides = above + below + to_right(value) + to_left(value)
    corners = to_left(above) + to_right(below)
    edge = 2.0 * FAC - 1.0
    return mean * value + (edge * (4.0 * value - sides) + (2.0 * value - corners)) * (
        1.0 / (FAC * FAC)
    )


def second_kernel(grid, blocks, got_ref, mean_ref, factor_ref, value_ref, slots_ref, line_ref):
    groups, tiles = grid
    high = factor_ref.shape[1] // LANES
    for side in range(2):
        for m in range(high // 2):
            line = None
            for g in range(side, groups, 2):
                part = jnp.sum(
                    got_ref[g * tiles : (g + 1) * tiles, m * LANES : (m + 1) * LANES],
                    axis=0,
                    keepdims=True,
                )
                line = part if line is None else line + part
            at = side * (high // 2) + m
            value_ref[at : at + 1, :] = line
    rest = interleave(*pairs(got_ref, (high // 2) * LANES, line_ref))
    coarse = rest - MIX * coarse_operator(value_ref[...], mean_ref[...], grid, blocks)
    terms = two_products(coarse, factor_ref)
    for m, term in enumerate(terms):
        slots_ref[2 * m : 2 * m + 1, :] = term
        slots_ref[2 * m + 1 : 2 * m + 2, :] = shift(term, LANES // 2, 1)


def prolong_line(line, first, shape):
    index = jnp.broadcast_to(first + lane_iota(shape) // FAC, shape)
    return gather_lanes(jnp.broadcast_to(line, shape), index)


def last_kernel(
    grid, got_ref, value_ref, rhs_ref, diag_ref, weight_ref, smooth_ref, out_ref, field_ref
):
    groups, tiles = grid
    g, t = lax.axis_index("grp"), lax.axis_index("tile")
    rows, cols = out_ref.shape
    block_rows, per_row = rows // FAC, cols // FAC
    here = block_rows * per_row
    inside = inside_mask(grid, rows, cols)
    up, down = jnp.maximum(g - 1, 0), jnp.minimum(g + 1, groups - 1)
    left, right = jnp.maximum(t - 1, 0), jnp.minimum(t + 1, tiles - 1)

    def line_of(device):
        return value_ref[pl.ds(device * here // LANES, 1), :], lax.rem(device * here, LANES)

    bands = [(a * FAC, FAC, g, a) for a in range(block_rows)]
    bands += [(rows, HALO, down, 0), (rows + HALO, HALO, up, block_rows - 1)]
    for start, height, group, a in bands:
        shape = (SUB, LANES)
        line, at = line_of(group * tiles + t)
        parts = [
            prolong_line(line, at + a * per_row + q * (LANES // FAC), shape)
            for q in range(cols // LANES)
        ]
        line, at = line_of(group * tiles + right)
        beside = gather_lanes(
            jnp.broadcast_to(line, shape), jnp.full(shape, at + a * per_row, jnp.int32)
        )
        line, at = line_of(group * tiles + left)
        other = gather_lanes(
            jnp.broadcast_to(line, shape),
            jnp.full(shape, at + (a + 1) * per_row - 1, jnp.int32),
        )
        parts.append(jnp.where(lane_iota(shape) < LANES // 2, beside, other))
        for low in range(start, start + height, SUB):
            for q, part in enumerate(parts):
                field_ref[low : low + SUB, q * LANES : (q + 1) * LANES] = part
    field = jnp.where(inside, smooth_ref[...] + MIX * field_ref[...], 0.0)
    rhs = rhs_ref[...]
    weight = weight_ref[...]
    rest = rhs - (6.0 + diag_ref[...]) * field + neighbour_sum(field)
    smooth = weight * rest
    for _ in range(SWEEPS - 1):
        smooth = (1.0 - OMEGA) * smooth + weight * (rest + neighbour_sum(smooth))
    line = MIX * jnp.sum(got_ref[...], axis=0, keepdims=True)
    for a in range(block_rows):
        for q in range(cols // LANES):
            part = prolong_line(line, a * per_row + q * (LANES // FAC), (SUB, LANES))
            for low in range(a * FAC, (a + 1) * FAC, SUB):
                where = (slice(low, low + SUB), slice(q * LANES, (q + 1) * LANES))
                out_ref[where] = field[where] + smooth[where] + part


def shards(right_side, diagonal, inverse_factor):
    groups, tiles = lax.axis_size("grp"), lax.axis_size("tile")
    grid = (groups, tiles)
    count = groups * tiles
    rows, cols = right_side.shape
    points = inverse_factor.shape[1]
    high = points // LANES
    blocks = (rows // FAC, cols // FAC)
    everyone = ("grp", "tile")
    swap = [(i, i ^ 1) for i in range(groups)]
    g = lax.axis_index("grp")

    width = 2 * rows * HALO + LANES
    edge = (2 * HALO, cols)
    slots, edge_a, edge_b = call(
        functools.partial(start_kernel, grid), [(count, width), edge, edge], 2
    )(right_side, diagonal)
    near = lax.ppermute(edge_a, "grp", swap)
    if groups > 2:
        across = [(i, i + 1) for i in range(1, groups - 1, 2)]
        across += [(j, i) for i, j in across]
        far = lax.ppermute(edge_b, "grp", across)
        below = jnp.where(g % 2 == 0, near, far)
        above = jnp.where(g % 2 == 0, far, near)
    else:
        below, above = near, near
    got = lax.all_to_all(slots, everyone, 0, 0, tiled=True)

    half = (high // 2, LANES)
    keep, send, mean = call(first_kernel, [half, half, (high, LANES)], 2, [(count, LANES)])(
        got, inverse_factor
    )
    came = lax.ppermute(send, "grp", swap)
    wide = (rows + 2 * HALO, cols + LANES)
    rhs, diag, weight, smooth, coarse = call(
        functools.partial(smooth_kernel, grid), [wide] * 4 + [(SUB, LANES)], 5,
        [(2 * rows * HALO // LANES, count, LANES)],
    )(got, right_side, diagonal, below, above)
    (slots,) = call(spread_kernel, [(count, points // 2 + LANES)], 3)(keep, came, coarse)
    got = lax.all_to_all(slots, everyone, 0, 0, tiled=True)

    value, slots = call(
        functools.partial(second_kernel, grid, blocks), [(high, LANES), (count, LANES)], 3,
        [(count, LANES)],
    )(got, mean, inverse_factor)
    got = lax.all_to_all(slots, everyone, 0, 0, tiled=True)

    return pl.pallas_call(
        functools.partial(last_kernel, grid),
        out_shape=jax.ShapeDtypeStruct((rows, cols), jnp.float32),
        in_specs=[VMEM] * 6,
        out_specs=VMEM,
        scratch_shapes=[pltpu.VMEM(wide, jnp.float32)],
    )(got, value, rhs, diag, weight, smooth)


def solution(mesh):
    placed = (P("grp", "tile"), P("grp", "tile"), P(("grp", "tile"), None))
    return jax.shard_map(
        shards, mesh=mesh, in_specs=placed, out_specs=P("grp", "tile"), check_vma=False
    )
```

```python
import functools

import jax
import jax.numpy as jnp
from jax import lax
from jax.experimental import pallas as pl
from jax.experimental.pallas import tpu as pltpu
from jax.sharding import PartitionSpec as P

FAC = 16
SWEEPS = 4
OMEGA = 0.8
MIX = 0.5
LANES = 128
SUB = 8
HALO = 8

VMEM = pl.BlockSpec(memory_space=pltpu.VMEM)


LIMIT = 8 * 1024 * 1024


def call(body, shapes, count, scratch=()):
    return pl.pallas_call(
        body,
        out_shape=[jax.ShapeDtypeStruct(s, jnp.float32) for s in shapes],
        in_specs=[VMEM] * count,
        out_specs=[VMEM] * len(shapes),
        scratch_shapes=[pltpu.VMEM(s, jnp.float32) for s in scratch],
        compiler_params=pltpu.CompilerParams(vmem_limit_bytes=LIMIT),
    )


def lane_iota(shape):
    return lax.broadcasted_iota(jnp.int32, shape, len(shape) - 1)


def row_iota(shape):
    return lax.broadcasted_iota(jnp.int32, shape, 0)


def shift(x, by, axis):
    return pltpu.roll(x, by % x.shape[axis], axis)


def neighbour_sum(x):
    above, below = shift(x, 1, 0), shift(x, -1, 0)
    return above + below + shift(x + above, -1, 1) + shift(x + below, 1, 1)


def gather_lanes(x, index):
    return jnp.take_along_axis(x, index, axis=1)


def pack_lanes(strip, first):
    step = LANES // HALO
    parts = []
    for at in range(0, strip.shape[0], step):
        piece = strip[at : at + step]
        lane, row = lane_iota(piece.shape), row_iota(piece.shape)
        piece = gather_lanes(piece, first + lax.rem(lane, HALO))
        piece = jnp.where(lane // HALO == row, piece, 0.0)
        parts.append(jnp.sum(piece, axis=0, keepdims=True))
    return parts


def start_kernel(grid, rhs_ref, diag_ref, slots_ref, edge_a_ref, edge_b_ref):
    groups, tiles = grid
    g, t = lax.axis_index("grp"), lax.axis_index("tile")
    rows, cols = rhs_ref.shape
    count = groups * tiles
    per_row = cols // FAC
    even = lax.rem(g, 2) == 0
    for at, ref in ((0, rhs_ref), (HALO, diag_ref)):
        first, last = ref[:HALO, :], ref[rows - HALO :, :]
        edge_a_ref[at : at + HALO, :] = jnp.where(even, last, first)
        if groups > 2:
            edge_b_ref[at : at + HALO, :] = jnp.where(even, first, last)
    sums = []
    for ref in (rhs_ref, diag_ref):
        for a in range(rows // FAC):
            sums.append(jnp.sum(ref[a * FAC : (a + 1) * FAC, :], axis=0, keepdims=True))
    tall = jnp.concatenate(sums + [jnp.zeros((SUB - len(sums), cols), jnp.float32)], axis=0)
    pick = (
        lax.broadcasted_iota(jnp.int32, (cols, LANES), 0) // FAC
        == lax.rem(lane_iota((cols, LANES)), per_row)
    ).astype(jnp.float32)
    means = jnp.dot(
        tall, pick, precision=lax.Precision.HIGHEST, preferred_element_type=jnp.float32
    ) * (1.0 / (FAC * FAC))
    group_of = lane_iota((1, LANES)) // per_row
    coarse = jnp.zeros((1, LANES), jnp.float32)
    for k in range(LANES // per_row):
        coarse = jnp.where(group_of == k, means[k : k + 1, :], coarse)
    to_left = lax.rem(row_iota((count, LANES)), tiles) < t
    lines = []
    for ref in (rhs_ref, diag_ref):
        left = pack_lanes(ref[:, :LANES], 0)
        right = pack_lanes(ref[:, cols - LANES :], LANES - HALO)
        lines += [jnp.where(to_left, one, two) for one, two in zip(left, right)]
    lines.append(jnp.broadcast_to(coarse, (count, LANES)))
    for k, line in enumerate(lines):
        slots_ref[pl.ds(k, count, stride=len(lines)), :] = line


def two_products(vector, factor_ref):
    high = factor_ref.shape[1] // LANES
    total = None
    for m in range(high):
        term = factor_ref[:, m * LANES : (m + 1) * LANES] * vector[m : m + 1, :]
        total = term if total is None else total + term
    inner = jnp.sum(total, axis=1, keepdims=True)
    return [
        jnp.sum(factor_ref[:, m * LANES : (m + 1) * LANES] * inner, axis=0, keepdims=True)
        for m in range(high)
    ]


def interleave(even, odd):
    return jnp.where(lane_iota(even.shape) < LANES // 2, even, odd)


def pairs(ref, line, width):
    count = ref.shape[0] // width
    return [
        ref[pl.ds(line + side * width, count // 2, stride=2 * width), :] for side in range(2)
    ]


def first_kernel(width, got_ref, factor_ref, keep_ref, send_ref, mean_ref):
    high = factor_ref.shape[1] // LANES
    even, odd = pairs(got_ref, width - 1, width)
    half = LANES // 2
    mean_ref[...] = interleave(shift(even, half, 1), odd)
    terms = two_products(interleave(even, shift(odd, half, 1)), factor_ref)
    own = lax.rem(lax.axis_index("grp"), 2) == 0
    for m in range(high // 2):
        low, top = terms[m], terms[m + high // 2]
        keep_ref[m : m + 1, :] = jnp.where(own, low, top)
        send_ref[m : m + 1, :] = jnp.where(own, top, low)


def inside_mask(grid, rows, cols):
    groups, tiles = grid
    g, t = lax.axis_index("grp"), lax.axis_index("tile")
    shape = (rows + 2 * HALO, cols + LANES)
    row, lane = row_iota(shape), lane_iota(shape)
    row_ok = (row < rows) | ((row < rows + HALO) & (g < groups - 1)) | ((row >= rows + HALO) & (g > 0))
    lane_ok = (
        (lane < cols)
        | ((lane < cols + HALO) & (t < tiles - 1))
        | ((lane >= cols + LANES - HALO) & (t > 0))
    )
    return row_ok & lane_ok


def unpack_lanes(got_ref, line, rows):
    step = LANES // HALO
    shape = (step, LANES)
    index = row_iota(shape) * HALO + lax.rem(lane_iota(shape), HALO)
    parts = []
    for k in range(rows // step):
        piece = jnp.broadcast_to(got_ref[pl.ds(line + k, 1), :], shape)
        parts.append(gather_lanes(piece, index))
    return jnp.concatenate(parts, axis=0)


def smooth_kernel(
    grid, width, got_ref, rhs_ref, diag_ref, below_ref, above_ref,
    rhs_out, diag_out, weight_out, smooth_out, coarse_out,
):
    groups, tiles = grid
    g, t = lax.axis_index("grp"), lax.axis_index("tile")
    rows, cols = rhs_ref.shape
    up, down = jnp.maximum(g - 1, 0), jnp.minimum(g + 1, groups - 1)
    left, right = jnp.maximum(t - 1, 0), jnp.minimum(t + 1, tiles - 1)
    inside = inside_mask(grid, rows, cols)
    at = 0
    for ref, out, edge in ((rhs_ref, rhs_out, 0), (diag_ref, diag_out, HALO)):
        out[:rows, :cols] = ref[...]
        out[rows : rows + HALO, :cols] = below_ref[edge : edge + HALO, :]
        out[rows + HALO :, :cols] = above_ref[edge : edge + HALO, :]
        sides = []
        for column in (right, left):
            mid = unpack_lanes(got_ref, (g * tiles + column) * width + at, rows)
            low = unpack_lanes(got_ref, (down * tiles + column) * width + at, rows)[:HALO]
            top = unpack_lanes(got_ref, (up * tiles + column) * width + at, rows)[rows - HALO :]
            sides.append(jnp.concatenate([mid, low, top], axis=0))
        lane = lane_iota(sides[0].shape)
        side = jnp.where(lane < HALO, sides[0], 0.0)
        side = jnp.where(lane >= LANES - HALO, sides[1], side)
        out[:, cols:] = side
        at += rows * HALO // LANES
    rhs = jnp.where(inside, rhs_out[...], 0.0)
    diag = jnp.where(inside, diag_out[...], 0.0)
    rhs_out[...] = rhs
    diag_out[...] = diag
    weight = jnp.where(inside, OMEGA / (6.0 + diag), 0.0)
    weight_out[...] = weight
    smooth = weight * rhs
    for _ in range(SWEEPS - 1):
        smooth = (1.0 - OMEGA) * smooth + weight * (rhs + neighbour_sum(smooth))
    smooth_out[...] = smooth
    left_over = (rhs - (6.0 + diag) * smooth + neighbour_sum(smooth))[:rows, :cols]
    per_row = cols // FAC
    sums = [
        jnp.sum(left_over[a * FAC : (a + 1) * FAC], axis=0, keepdims=True)
        for a in range(rows // FAC)
    ]
    tall = jnp.concatenate(sums + [jnp.zeros((SUB - len(sums), cols), jnp.float32)], axis=0)
    pick = (
        lax.broadcasted_iota(jnp.int32, (cols, LANES), 0) // FAC
        == lax.rem(lane_iota((cols, LANES)), per_row)
    ).astype(jnp.float32)
    means = jnp.dot(
        tall, pick, precision=lax.Precision.HIGHEST, preferred_element_type=jnp.float32
    ) * (1.0 / (FAC * FAC))
    group_of = lax.rem(lane_iota((1, LANES)) // per_row, rows // FAC)
    coarse = jnp.zeros((1, LANES), jnp.float32)
    for a in range(rows // FAC):
        coarse = jnp.where(group_of == a, means[a : a + 1, :], coarse)
    coarse_out[...] = jnp.broadcast_to(coarse, (SUB, LANES))


def spread_kernel(keep_ref, came_ref, coarse_ref, slots_ref):
    high = keep_ref.shape[0]
    width = high + 1
    half = keep_ref[...] + came_ref[...]
    for device in range(slots_ref.shape[0] // width):
        slots_ref[device * width : device * width + high, :] = half
        slots_ref[device * width + high : (device + 1) * width, :] = coarse_ref[:1, :]


def coarse_operator(value, mean, grid, blocks):
    groups, tiles = grid
    block_rows, per_row = blocks
    here = block_rows * per_row
    shape = value.shape
    lane, row = lane_iota(shape), row_iota(shape)
    device = row * (LANES // here) + lane // here
    a = lax.rem(lane, here) // per_row
    b = lax.rem(lane, per_row)
    tile, group = lax.rem(device, tiles), device // tiles
    per_line = tiles * here // LANES

    def to_right(x):
        near = shift(x, 1, 1)
        far = shift(x, here - per_row + 1, 1)
        far = jnp.where(lane < here, shift(far, 1, 0), far)
        return jnp.where(b > 0, near, jnp.where(tile > 0, far, 0.0))

    def to_left(x):
        near = shift(x, -1, 1)
        far = shift(x, -(here - per_row + 1), 1)
        far = jnp.where(lane >= LANES - here, shift(far, -1, 0), far)
        return jnp.where(b < per_row - 1, near, jnp.where(tile < tiles - 1, far, 0.0))

    def to_below(x):
        near = shift(x, per_row, 1)
        far = shift(shift(x, -(here - per_row), 1), per_line, 0)
        return jnp.where(a > 0, near, jnp.where(group > 0, far, 0.0))

    def to_above(x):
        near = shift(x, -per_row, 1)
        far = shift(shift(x, here - per_row, 1), -per_line, 0)
        return jnp.where(a < block_rows - 1, near, jnp.where(group < groups - 1, far, 0.0))

    above, below = to_below(value), to_above(value)
    sides = above + below + to_right(value) + to_left(value)
    corners = to_left(above) + to_right(below)
    edge = 2.0 * FAC - 1.0
    return mean * value + (edge * (4.0 * value - sides) + (2.0 * value - corners)) * (
        1.0 / (FAC * FAC)
    )


def second_kernel(grid, blocks, got_ref, mean_ref, factor_ref, value_ref, slots_ref):
    groups, tiles = grid
    high = factor_ref.shape[1] // LANES // 2
    width = high + 1
    for side in range(2):
        total = None
        for g in range(side, groups, 2):
            for device in range(g * tiles, (g + 1) * tiles):
                part = got_ref[device * width : device * width + high, :]
                total = part if total is None else total + part
        value_ref[side * high : (side + 1) * high, :] = total
    rest = interleave(*pairs(got_ref, high, width))
    coarse = rest - MIX * coarse_operator(value_ref[...], mean_ref[...], grid, blocks)
    terms = two_products(coarse, factor_ref)
    for m, term in enumerate(terms):
        slots_ref[2 * m : 2 * m + 1, :] = term
        slots_ref[2 * m + 1 : 2 * m + 2, :] = shift(term, LANES // 2, 1)


def prolong_line(line, first, shape):
    index = jnp.broadcast_to(first + lane_iota(shape) // FAC, shape)
    return gather_lanes(jnp.broadcast_to(line, shape), index)


def resmooth_kernel(
    grid, value_ref, rhs_ref, diag_ref, weight_ref, smooth_ref, base_ref, field_ref
):
    groups, tiles = grid
    g, t = lax.axis_index("grp"), lax.axis_index("tile")
    rows, cols = base_ref.shape
    block_rows, per_row = rows // FAC, cols // FAC
    here = block_rows * per_row
    inside = inside_mask(grid, rows, cols)
    up, down = jnp.maximum(g - 1, 0), jnp.minimum(g + 1, groups - 1)
    left, right = jnp.maximum(t - 1, 0), jnp.minimum(t + 1, tiles - 1)

    def line_of(device):
        return value_ref[pl.ds(device * here // LANES, 1), :], lax.rem(device * here, LANES)

    bands = [(a * FAC, FAC, g, a) for a in range(block_rows)]
    bands += [(rows, HALO, down, 0), (rows + HALO, HALO, up, block_rows - 1)]
    for start, height, group, a in bands:
        shape = (SUB, LANES)
        line, at = line_of(group * tiles + t)
        parts = [
            prolong_line(line, at + a * per_row + q * (LANES // FAC), shape)
            for q in range(cols // LANES)
        ]
        line, at = line_of(group * tiles + right)
        beside = gather_lanes(
            jnp.broadcast_to(line, shape), jnp.full(shape, at + a * per_row, jnp.int32)
        )
        line, at = line_of(group * tiles + left)
        other = gather_lanes(
            jnp.broadcast_to(line, shape),
            jnp.full(shape, at + (a + 1) * per_row - 1, jnp.int32),
        )
        parts.append(jnp.where(lane_iota(shape) < LANES // 2, beside, other))
        for low in range(start, start + height, SUB):
            for q, part in enumerate(parts):
                field_ref[low : low + SUB, q * LANES : (q + 1) * LANES] = part
    field = jnp.where(inside, smooth_ref[...] + MIX * field_ref[...], 0.0)
    rhs = rhs_ref[...]
    weight = weight_ref[...]
    rest = rhs - (6.0 + diag_ref[...]) * field + neighbour_sum(field)
    smooth = weight * rest
    for _ in range(SWEEPS - 1):
        smooth = (1.0 - OMEGA) * smooth + weight * (rest + neighbour_sum(smooth))
    base_ref[...] = field[:rows, :cols] + smooth[:rows, :cols]


def last_kernel(got_ref, base_ref, out_ref):
    rows, cols = out_ref.shape
    per_row = cols // FAC
    line = MIX * jnp.sum(got_ref[...], axis=0, keepdims=True)
    for a in range(rows // FAC):
        for q in range(cols // LANES):
            part = prolong_line(line, a * per_row + q * (LANES // FAC), (SUB, LANES))
            for low in range(a * FAC, (a + 1) * FAC, SUB):
                where = (slice(low, low + SUB), slice(q * LANES, (q + 1) * LANES))
                out_ref[where] = base_ref[where] + part


def shards(right_side, diagonal, inverse_factor):
    groups, tiles = lax.axis_size("grp"), lax.axis_size("tile")
    grid = (groups, tiles)
    count = groups * tiles
    rows, cols = right_side.shape
    points = inverse_factor.shape[1]
    high = points // LANES
    blocks = (rows // FAC, cols // FAC)
    everyone = ("grp", "tile")
    swap = [(i, i ^ 1) for i in range(groups)]
    g = lax.axis_index("grp")

    def exchange(slots):
        lines = slots.shape[0] // count
        got = lax.all_to_all(slots.reshape(count, lines * LANES), everyone, 0, 0, tiled=True)
        return got.reshape(count * lines, LANES)

    width = 2 * rows * HALO // LANES + 1
    edge = (2 * HALO, cols)
    slots, edge_a, edge_b = call(
        functools.partial(start_kernel, grid), [(count * width, LANES), edge, edge], 2
    )(right_side, diagonal)
    near = lax.ppermute(edge_a, "grp", swap)
    if groups > 2:
        across = [(i, i + 1) for i in range(1, groups - 1, 2)]
        across += [(j, i) for i, j in across]
        far = lax.ppermute(edge_b, "grp", across)
        below = jnp.where(g % 2 == 0, near, far)
        above = jnp.where(g % 2 == 0, far, near)
    else:
        below, above = near, near
    got = exchange(slots)

    half = (high // 2, LANES)
    keep, send, mean = call(
        functools.partial(first_kernel, width), [half, half, (high, LANES)], 2
    )(got, inverse_factor)
    came = lax.ppermute(send, "grp", swap)
    wide = (rows + 2 * HALO, cols + LANES)
    rhs, diag, weight, smooth, coarse = call(
        functools.partial(smooth_kernel, grid, width), [wide] * 4 + [(SUB, LANES)], 5
    )(got, right_side, diagonal, below, above)
    (slots,) = call(spread_kernel, [(count * (high // 2 + 1), LANES)], 3)(keep, came, coarse)
    got = exchange(slots)

    value, slots = call(
        functools.partial(second_kernel, grid, blocks), [(high, LANES), (count, LANES)], 3
    )(got, mean, inverse_factor)
    got = exchange(slots)
    (base,) = call(
        functools.partial(resmooth_kernel, grid), [(rows, cols)], 5, [wide]
    )(value, rhs, diag, weight, smooth)
    (field,) = call(last_kernel, [(rows, cols)], 2)(got, base)
    return field


def solution(mesh):
    placed = (P("grp", "tile"), P("grp", "tile"), P(("grp", "tile"), None))
    return jax.shard_map(
        shards, mesh=mesh, in_specs=placed, out_specs=P("grp", "tile"), check_vma=False
    )
```

```python
import functools

import jax
import jax.numpy as jnp
from jax import lax
from jax.experimental import pallas as pl
from jax.experimental.pallas import tpu as pltpu
from jax.sharding import PartitionSpec as P

FAC = 16
SWEEPS = 4
OMEGA = 0.8
MIX = 0.5
LANES = 128
SUB = 8
HALO = 8

VMEM = pl.BlockSpec(memory_space=pltpu.VMEM)


LIMIT = 8 * 1024 * 1024


def call(body, shapes, count, scratch=()):
    return pl.pallas_call(
        body,
        out_shape=[jax.ShapeDtypeStruct(s, jnp.float32) for s in shapes],
        in_specs=[VMEM] * count,
        out_specs=[VMEM] * len(shapes),
        scratch_shapes=[pltpu.VMEM(s, jnp.float32) for s in scratch],
        compiler_params=pltpu.CompilerParams(vmem_limit_bytes=LIMIT),
    )


def lane_iota(shape):
    return lax.broadcasted_iota(jnp.int32, shape, len(shape) - 1)


def row_iota(shape):
    return lax.broadcasted_iota(jnp.int32, shape, 0)


def shift(x, by, axis):
    return pltpu.roll(x, by % x.shape[axis], axis)


def neighbour_sum(x):
    above, below = shift(x, 1, 0), shift(x, -1, 0)
    return above + below + shift(x + above, -1, 1) + shift(x + below, 1, 1)


def gather_lanes(x, index):
    return jnp.take_along_axis(x, index, axis=1)


def pack_lanes(strip, first):
    step = LANES // HALO
    parts = []
    for at in range(0, strip.shape[0], step):
        piece = strip[at : at + step]
        lane, row = lane_iota(piece.shape), row_iota(piece.shape)
        piece = gather_lanes(piece, first + lax.rem(lane, HALO))
        piece = jnp.where(lane // HALO == row, piece, 0.0)
        parts.append(jnp.sum(piece, axis=0, keepdims=True))
    return parts


def start_kernel(
    grid, rhs_in, diag_in, factor_in, slots_ref, rhs_ref, diag_ref, factor_ref, *rest
):
    edge_refs, sems = rest[:-1], rest[-1]
    loads = [
        pltpu.make_async_copy(source, target, sems.at[k])
        for k, (source, target) in enumerate(
            ((rhs_in, rhs_ref), (diag_in, diag_ref), (factor_in, factor_ref))
        )
    ]
    for load in loads:
        load.start()
    groups, tiles = grid
    g, t = lax.axis_index("grp"), lax.axis_index("tile")
    rows, cols = rhs_ref.shape
    count = groups * tiles
    per_row = cols // FAC
    even = lax.rem(g, 2) == 0
    pick = (
        lax.broadcasted_iota(jnp.int32, (cols, LANES), 0) // FAC
        == lax.rem(lane_iota((cols, LANES)), per_row)
    ).astype(jnp.float32)
    loads[0].wait()
    loads[1].wait()
    for at, ref in ((0, rhs_ref), (HALO, diag_ref)):
        first, last = ref[:HALO, :], ref[rows - HALO :, :]
        for edge_ref, odd in zip(edge_refs, (False, True)):
            edge_ref[at : at + HALO, :] = jnp.where(even != odd, last, first)
    sums = []
    for ref in (rhs_ref, diag_ref):
        for a in range(rows // FAC):
            sums.append(jnp.sum(ref[a * FAC : (a + 1) * FAC, :], axis=0, keepdims=True))
    tall = jnp.concatenate(sums + [jnp.zeros((SUB - len(sums), cols), jnp.float32)], axis=0)
    means = jnp.dot(
        tall, pick, precision=lax.Precision.HIGHEST, preferred_element_type=jnp.float32
    ) * (1.0 / (FAC * FAC))
    group_of = lane_iota((1, LANES)) // per_row
    coarse = jnp.zeros((1, LANES), jnp.float32)
    for k in range(LANES // per_row):
        coarse = jnp.where(group_of == k, means[k : k + 1, :], coarse)
    to_left = lax.rem(row_iota((count, LANES)), tiles) < t
    lines = []
    for ref in (rhs_ref, diag_ref):
        left = pack_lanes(ref[:, :LANES], 0)
        right = pack_lanes(ref[:, cols - LANES :], LANES - HALO)
        lines += [jnp.where(to_left, one, two) for one, two in zip(left, right)]
    lines.append(jnp.broadcast_to(coarse, (count, LANES)))
    for k, line in enumerate(lines):
        slots_ref[pl.ds(k, count, stride=len(lines)), :] = line
    loads[2].wait()


def two_products(vector, factor_ref):
    high = factor_ref.shape[1] // LANES
    total = None
    for m in range(high):
        term = factor_ref[:, m * LANES : (m + 1) * LANES] * vector[m : m + 1, :]
        total = term if total is None else total + term
    inner = jnp.sum(total, axis=1, keepdims=True)
    return [
        jnp.sum(factor_ref[:, m * LANES : (m + 1) * LANES] * inner, axis=0, keepdims=True)
        for m in range(high)
    ]


def interleave(even, odd):
    return jnp.where(lane_iota(even.shape) < LANES // 2, even, odd)


def pairs(ref, line, width):
    count = ref.shape[0] // width
    return [
        ref[pl.ds(line + side * width, count // 2, stride=2 * width), :] for side in range(2)
    ]


def first_kernel(width, got_ref, factor_ref, keep_ref, send_ref, mean_ref):
    high = factor_ref.shape[1] // LANES
    even, odd = pairs(got_ref, width - 1, width)
    half = LANES // 2
    mean_ref[...] = interleave(shift(even, half, 1), odd)
    terms = two_products(interleave(even, shift(odd, half, 1)), factor_ref)
    own = lax.rem(lax.axis_index("grp"), 2) == 0
    for m in range(high // 2):
        low, top = terms[m], terms[m + high // 2]
        keep_ref[m : m + 1, :] = jnp.where(own, low, top)
        send_ref[m : m + 1, :] = jnp.where(own, top, low)


def inside_mask(grid, rows, cols):
    groups, tiles = grid
    g, t = lax.axis_index("grp"), lax.axis_index("tile")
    shape = (rows + 2 * HALO, cols + LANES)
    row, lane = row_iota(shape), lane_iota(shape)
    row_ok = (row < rows) | ((row < rows + HALO) & (g < groups - 1)) | ((row >= rows + HALO) & (g > 0))
    lane_ok = (
        (lane < cols)
        | ((lane < cols + HALO) & (t < tiles - 1))
        | ((lane >= cols + LANES - HALO) & (t > 0))
    )
    return row_ok & lane_ok


def unpack_lanes(got_ref, line, rows):
    step = LANES // HALO
    shape = (step, LANES)
    index = row_iota(shape) * HALO + lax.rem(lane_iota(shape), HALO)
    parts = []
    for k in range(rows // step):
        piece = jnp.broadcast_to(got_ref[pl.ds(line + k, 1), :], shape)
        parts.append(gather_lanes(piece, index))
    return jnp.concatenate(parts, axis=0)


def smooth_kernel(
    grid, width, got_ref, rhs_ref, diag_ref, below_ref, above_ref,
    rhs_out, diag_out, weight_out, smooth_out, coarse_out,
):
    groups, tiles = grid
    g, t = lax.axis_index("grp"), lax.axis_index("tile")
    rows, cols = rhs_ref.shape
    up, down = jnp.maximum(g - 1, 0), jnp.minimum(g + 1, groups - 1)
    left, right = jnp.maximum(t - 1, 0), jnp.minimum(t + 1, tiles - 1)
    inside = inside_mask(grid, rows, cols)
    at = 0
    for ref, out, edge in ((rhs_ref, rhs_out, 0), (diag_ref, diag_out, HALO)):
        out[:rows, :cols] = ref[...]
        out[rows : rows + HALO, :cols] = below_ref[edge : edge + HALO, :]
        out[rows + HALO :, :cols] = above_ref[edge : edge + HALO, :]
        sides = []
        for column in (right, left):
            mid = unpack_lanes(got_ref, (g * tiles + column) * width + at, rows)
            low = unpack_lanes(got_ref, (down * tiles + column) * width + at, rows)[:HALO]
            top = unpack_lanes(got_ref, (up * tiles + column) * width + at, rows)[rows - HALO :]
            sides.append(jnp.concatenate([mid, low, top], axis=0))
        lane = lane_iota(sides[0].shape)
        side = jnp.where(lane < HALO, sides[0], 0.0)
        side = jnp.where(lane >= LANES - HALO, sides[1], side)
        out[:, cols:] = side
        at += rows * HALO // LANES
    rhs = jnp.where(inside, rhs_out[...], 0.0)
    diag = jnp.where(inside, diag_out[...], 0.0)
    rhs_out[...] = rhs
    diag_out[...] = diag
    weight = jnp.where(inside, OMEGA / (6.0 + diag), 0.0)
    weight_out[...] = weight
    smooth = weight * rhs
    for _ in range(SWEEPS - 1):
        smooth = (1.0 - OMEGA) * smooth + weight * (rhs + neighbour_sum(smooth))
    smooth_out[...] = smooth
    left_over = (rhs - (6.0 + diag) * smooth + neighbour_sum(smooth))[:rows, :cols]
    per_row = cols // FAC
    sums = [
        jnp.sum(left_over[a * FAC : (a + 1) * FAC], axis=0, keepdims=True)
        for a in range(rows // FAC)
    ]
    tall = jnp.concatenate(sums + [jnp.zeros((SUB - len(sums), cols), jnp.float32)], axis=0)
    pick = (
        lax.broadcasted_iota(jnp.int32, (cols, LANES), 0) // FAC
        == lax.rem(lane_iota((cols, LANES)), per_row)
    ).astype(jnp.float32)
    means = jnp.dot(
        tall, pick, precision=lax.Precision.HIGHEST, preferred_element_type=jnp.float32
    ) * (1.0 / (FAC * FAC))
    group_of = lax.rem(lane_iota((1, LANES)) // per_row, rows // FAC)
    coarse = jnp.zeros((1, LANES), jnp.float32)
    for a in range(rows // FAC):
        coarse = jnp.where(group_of == a, means[a : a + 1, :], coarse)
    coarse_out[...] = jnp.broadcast_to(coarse, (SUB, LANES))


def spread_kernel(keep_ref, came_ref, coarse_ref, slots_ref):
    high = keep_ref.shape[0]
    width = high + 1
    half = keep_ref[...] + came_ref[...]
    for device in range(slots_ref.shape[0] // width):
        slots_ref[device * width : device * width + high, :] = half
        slots_ref[device * width + high : (device + 1) * width, :] = coarse_ref[:1, :]


def coarse_operator(value, mean, grid, blocks):
    groups, tiles = grid
    block_rows, per_row = blocks
    here = block_rows * per_row
    shape = value.shape
    lane, row = lane_iota(shape), row_iota(shape)
    device = row * (LANES // here) + lane // here
    a = lax.rem(lane, here) // per_row
    b = lax.rem(lane, per_row)
    tile, group = lax.rem(device, tiles), device // tiles
    per_line = tiles * here // LANES

    def to_right(x):
        near = shift(x, 1, 1)
        far = shift(x, here - per_row + 1, 1)
        far = jnp.where(lane < here, shift(far, 1, 0), far)
        return jnp.where(b > 0, near, jnp.where(tile > 0, far, 0.0))

    def to_left(x):
        near = shift(x, -1, 1)
        far = shift(x, -(here - per_row + 1), 1)
        far = jnp.where(lane >= LANES - here, shift(far, -1, 0), far)
        return jnp.where(b < per_row - 1, near, jnp.where(tile < tiles - 1, far, 0.0))

    def to_below(x):
        near = shift(x, per_row, 1)
        far = shift(shift(x, -(here - per_row), 1), per_line, 0)
        return jnp.where(a > 0, near, jnp.where(group > 0, far, 0.0))

    def to_above(x):
        near = shift(x, -per_row, 1)
        far = shift(shift(x, here - per_row, 1), -per_line, 0)
        return jnp.where(a < block_rows - 1, near, jnp.where(group < groups - 1, far, 0.0))

    above, below = to_below(value), to_above(value)
    sides = above + below + to_right(value) + to_left(value)
    corners = to_left(above) + to_right(below)
    edge = 2.0 * FAC - 1.0
    return mean * value + (edge * (4.0 * value - sides) + (2.0 * value - corners)) * (
        1.0 / (FAC * FAC)
    )


def second_kernel(grid, blocks, got_ref, mean_ref, factor_ref, value_ref, slots_ref):
    groups, tiles = grid
    high = factor_ref.shape[1] // LANES // 2
    width = high + 1
    for side in range(2):
        total = None
        for g in range(side, groups, 2):
            for device in range(g * tiles, (g + 1) * tiles):
                part = got_ref[device * width : device * width + high, :]
                total = part if total is None else total + part
        value_ref[side * high : (side + 1) * high, :] = total
    rest = interleave(*pairs(got_ref, high, width))
    coarse = rest - MIX * coarse_operator(value_ref[...], mean_ref[...], grid, blocks)
    terms = two_products(coarse, factor_ref)
    for m, term in enumerate(terms):
        slots_ref[2 * m : 2 * m + 1, :] = term
        slots_ref[2 * m + 1 : 2 * m + 2, :] = shift(term, LANES // 2, 1)


def prolong_line(line, first, shape):
    index = jnp.broadcast_to(first + lane_iota(shape) // FAC, shape)
    return gather_lanes(jnp.broadcast_to(line, shape), index)


def resmooth_kernel(
    grid, value_ref, rhs_ref, diag_ref, weight_ref, smooth_ref, base_ref, field_ref
):
    groups, tiles = grid
    g, t = lax.axis_index("grp"), lax.axis_index("tile")
    rows, cols = base_ref.shape
    block_rows, per_row = rows // FAC, cols // FAC
    here = block_rows * per_row
    inside = inside_mask(grid, rows, cols)
    up, down = jnp.maximum(g - 1, 0), jnp.minimum(g + 1, groups - 1)
    left, right = jnp.maximum(t - 1, 0), jnp.minimum(t + 1, tiles - 1)

    def line_of(device):
        return value_ref[pl.ds(device * here // LANES, 1), :], lax.rem(device * here, LANES)

    bands = [(a * FAC, FAC, g, a) for a in range(block_rows)]
    bands += [(rows, HALO, down, 0), (rows + HALO, HALO, up, block_rows - 1)]
    for start, height, group, a in bands:
        shape = (SUB, LANES)
        line, at = line_of(group * tiles + t)
        parts = [
            prolong_line(line, at + a * per_row + q * (LANES // FAC), shape)
            for q in range(cols // LANES)
        ]
        line, at = line_of(group * tiles + right)
        beside = gather_lanes(
            jnp.broadcast_to(line, shape), jnp.full(shape, at + a * per_row, jnp.int32)
        )
        line, at = line_of(group * tiles + left)
        other = gather_lanes(
            jnp.broadcast_to(line, shape),
            jnp.full(shape, at + (a + 1) * per_row - 1, jnp.int32),
        )
        parts.append(jnp.where(lane_iota(shape) < LANES // 2, beside, other))
        for low in range(start, start + height, SUB):
            for q, part in enumerate(parts):
                field_ref[low : low + SUB, q * LANES : (q + 1) * LANES] = part
    field = jnp.where(inside, smooth_ref[...] + MIX * field_ref[...], 0.0)
    rhs = rhs_ref[...]
    weight = weight_ref[...]
    rest = rhs - (6.0 + diag_ref[...]) * field + neighbour_sum(field)
    smooth = weight * rest
    for _ in range(SWEEPS - 1):
        smooth = (1.0 - OMEGA) * smooth + weight * (rest + neighbour_sum(smooth))
    base_ref[...] = field[:rows, :cols] + smooth[:rows, :cols]


def last_kernel(got_ref, base_ref, out_ref):
    rows, cols = out_ref.shape
    per_row = cols // FAC
    line = MIX * jnp.sum(got_ref[...], axis=0, keepdims=True)
    for a in range(rows // FAC):
        for q in range(cols // LANES):
            part = prolong_line(line, a * per_row + q * (LANES // FAC), (SUB, LANES))
            for low in range(a * FAC, (a + 1) * FAC, SUB):
                where = (slice(low, low + SUB), slice(q * LANES, (q + 1) * LANES))
                out_ref[where] = base_ref[where] + part


def shards(right_side, diagonal, inverse_factor):
    groups, tiles = lax.axis_size("grp"), lax.axis_size("tile")
    grid = (groups, tiles)
    count = groups * tiles
    rows, cols = right_side.shape
    points = inverse_factor.shape[1]
    high = points // LANES
    blocks = (rows // FAC, cols // FAC)
    everyone = ("grp", "tile")
    swap = [(i, i ^ 1) for i in range(groups)]
    g = lax.axis_index("grp")

    def exchange(slots):
        lines = slots.shape[0] // count
        got = lax.all_to_all(slots.reshape(count, lines * LANES), everyone, 0, 0, tiled=True)
        return got.reshape(count * lines, LANES)

    width = 2 * rows * HALO // LANES + 1
    edge = (2 * HALO, cols)
    shapes = [(count * width, LANES), (rows, cols), (rows, cols), inverse_factor.shape]
    shapes += [edge] * (2 if groups > 2 else 1)
    slots, right_side, diagonal, inverse_factor, *edges = pl.pallas_call(
        functools.partial(start_kernel, grid),
        out_shape=[jax.ShapeDtypeStruct(s, jnp.float32) for s in shapes],
        in_specs=[pl.BlockSpec(memory_space=pltpu.HBM)] * 3,
        out_specs=[VMEM] * len(shapes),
        scratch_shapes=[pltpu.SemaphoreType.DMA((3,))],
        compiler_params=pltpu.CompilerParams(vmem_limit_bytes=LIMIT),
    )(
        *[
            pltpu.with_memory_space_constraint(x, pltpu.HBM)
            for x in (right_side, diagonal, inverse_factor)
        ]
    )
    near = lax.ppermute(edges[0], "grp", swap)
    if groups > 2:
        across = [(i, i + 1) for i in range(1, groups - 1, 2)]
        across += [(j, i) for i, j in across]
        far = lax.ppermute(edges[1], "grp", across)
        below = jnp.where(g % 2 == 0, near, far)
        above = jnp.where(g % 2 == 0, far, near)
    else:
        below, above = near, near
    got = exchange(slots)

    half = (high // 2, LANES)
    keep, send, mean = call(
        functools.partial(first_kernel, width), [half, half, (high, LANES)], 2
    )(got, inverse_factor)
    came = lax.ppermute(send, "grp", swap)
    wide = (rows + 2 * HALO, cols + LANES)
    rhs, diag, weight, smooth, coarse = call(
        functools.partial(smooth_kernel, grid, width), [wide] * 4 + [(SUB, LANES)], 5
    )(got, right_side, diagonal, below, above)
    (slots,) = call(spread_kernel, [(count * (high // 2 + 1), LANES)], 3)(keep, came, coarse)
    got = exchange(slots)

    value, slots = call(
        functools.partial(second_kernel, grid, blocks), [(high, LANES), (count, LANES)], 3
    )(got, mean, inverse_factor)
    got = exchange(slots)
    (base,) = call(
        functools.partial(resmooth_kernel, grid), [(rows, cols)], 5, [wide]
    )(value, rhs, diag, weight, smooth)
    (field,) = call(last_kernel, [(rows, cols)], 2)(got, base)
    return field


def solution(mesh):
    placed = (P("grp", "tile"), P("grp", "tile"), P(("grp", "tile"), None))
    return jax.shard_map(
        shards, mesh=mesh, in_specs=placed, out_specs=P("grp", "tile"), check_vma=False
    )
```

```python
import functools

import jax
import jax.numpy as jnp
from jax import lax
from jax.experimental import pallas as pl
from jax.experimental.pallas import tpu as pltpu
from jax.sharding import PartitionSpec as P

FAC = 16
SWEEPS = 4
OMEGA = 0.8
MIX = 0.5
LANES = 128
SUB = 8
HALO = 8

VMEM = pl.BlockSpec(memory_space=pltpu.VMEM)


LIMIT = 8 * 1024 * 1024


def call(body, shapes, count, scratch=()):
    return pl.pallas_call(
        body,
        out_shape=[jax.ShapeDtypeStruct(s, jnp.float32) for s in shapes],
        in_specs=[VMEM] * count,
        out_specs=[VMEM] * len(shapes),
        scratch_shapes=[pltpu.VMEM(s, jnp.float32) for s in scratch],
        compiler_params=pltpu.CompilerParams(vmem_limit_bytes=LIMIT),
    )


def lane_iota(shape):
    return lax.broadcasted_iota(jnp.int32, shape, len(shape) - 1)


def row_iota(shape):
    return lax.broadcasted_iota(jnp.int32, shape, 0)


def shift(x, by, axis):
    return pltpu.roll(x, by % x.shape[axis], axis)


def neighbour_sum(x):
    above, below = shift(x, 1, 0), shift(x, -1, 0)
    return above + below + shift(x + above, -1, 1) + shift(x + below, 1, 1)


def gather_lanes(x, index):
    return jnp.take_along_axis(x, index, axis=1)


def block_means(arrays):
    rows, cols = arrays[0].shape
    per_row = cols // FAC
    sums = [
        jnp.sum(x[a * FAC : (a + 1) * FAC], axis=0, keepdims=True)
        for x in arrays
        for a in range(rows // FAC)
    ]
    used = len(sums)
    high = jnp.concatenate(sums, axis=0)
    parts = []
    for _ in range(3):
        part = high.astype(jnp.bfloat16)
        parts.append(part.astype(jnp.float32))
        high = high - parts[-1]
    fill = -len(parts) * used % (2 * SUB)
    tall = jnp.concatenate(parts + [jnp.zeros((fill, cols), jnp.float32)], axis=0)
    pick = (
        lax.broadcasted_iota(jnp.int32, (cols, LANES), 0) // FAC
        == lax.rem(lane_iota((cols, LANES)), per_row)
    )
    line = jnp.dot(
        tall.astype(jnp.bfloat16),
        pick.astype(jnp.bfloat16),
        preferred_element_type=jnp.float32,
    )
    mine = lax.rem(row_iota(line.shape), used) == lax.rem(lane_iota(line.shape) // per_row, used)
    line = jnp.where(mine, line, 0.0)
    return jnp.sum(line, axis=0, keepdims=True) * (1.0 / (FAC * FAC))


def pack_lanes(strip, first):
    step = LANES // HALO
    parts = []
    for at in range(0, strip.shape[0], step):
        piece = strip[at : at + step]
        lane, row = lane_iota(piece.shape), row_iota(piece.shape)
        piece = gather_lanes(piece, first + lax.rem(lane, HALO))
        piece = jnp.where(lane // HALO == row, piece, 0.0)
        parts.append(jnp.sum(piece, axis=0, keepdims=True))
    return parts


def start_kernel(
    grid, rhs_in, diag_in, factor_in, slots_ref, rhs_ref, diag_ref, factor_ref, *rest
):
    edge_refs, sems = rest[:-1], rest[-1]
    loads = [
        pltpu.make_async_copy(source, target, sems.at[k])
        for k, (source, target) in enumerate(
            ((rhs_in, rhs_ref), (diag_in, diag_ref), (factor_in, factor_ref))
        )
    ]
    for load in loads:
        load.start()
    groups, tiles = grid
    g, t = lax.axis_index("grp"), lax.axis_index("tile")
    rows, cols = rhs_ref.shape
    count = groups * tiles
    even = lax.rem(g, 2) == 0
    loads[0].wait()
    loads[1].wait()
    for at, ref in ((0, rhs_ref), (HALO, diag_ref)):
        first, last = ref[:HALO, :], ref[rows - HALO :, :]
        for edge_ref, odd in zip(edge_refs, (False, True)):
            edge_ref[at : at + HALO, :] = jnp.where(even != odd, last, first)
    coarse = block_means([rhs_ref[...], diag_ref[...]])
    to_left = lax.rem(row_iota((count, LANES)), tiles) < t
    lines = []
    for ref in (rhs_ref, diag_ref):
        left = pack_lanes(ref[:, :LANES], 0)
        right = pack_lanes(ref[:, cols - LANES :], LANES - HALO)
        lines += [jnp.where(to_left, one, two) for one, two in zip(left, right)]
    lines.append(jnp.broadcast_to(coarse, (count, LANES)))
    for k, line in enumerate(lines):
        slots_ref[pl.ds(k, count, stride=len(lines)), :] = line
    loads[2].wait()


def two_products(vector, factor_ref):
    high = factor_ref.shape[1] // LANES
    total = None
    for m in range(high):
        term = factor_ref[:, m * LANES : (m + 1) * LANES] * vector[m : m + 1, :]
        total = term if total is None else total + term
    inner = jnp.sum(total, axis=1, keepdims=True)
    return [
        jnp.sum(factor_ref[:, m * LANES : (m + 1) * LANES] * inner, axis=0, keepdims=True)
        for m in range(high)
    ]


def interleave(even, odd):
    return jnp.where(lane_iota(even.shape) < LANES // 2, even, odd)


def pairs(ref, line, width):
    count = ref.shape[0] // width
    return [
        ref[pl.ds(line + side * width, count // 2, stride=2 * width), :] for side in range(2)
    ]


def first_kernel(width, got_ref, factor_ref, keep_ref, send_ref, mean_ref):
    high = factor_ref.shape[1] // LANES
    even, odd = pairs(got_ref, width - 1, width)
    half = LANES // 2
    mean_ref[...] = interleave(shift(even, half, 1), odd)
    terms = two_products(interleave(even, shift(odd, half, 1)), factor_ref)
    own = lax.rem(lax.axis_index("grp"), 2) == 0
    for m in range(high // 2):
        low, top = terms[m], terms[m + high // 2]
        keep_ref[m : m + 1, :] = jnp.where(own, low, top)
        send_ref[m : m + 1, :] = jnp.where(own, top, low)


def inside_mask(grid, rows, cols):
    groups, tiles = grid
    g, t = lax.axis_index("grp"), lax.axis_index("tile")
    shape = (rows + 2 * HALO, cols + LANES)
    row, lane = row_iota(shape), lane_iota(shape)
    row_ok = (row < rows) | ((row < rows + HALO) & (g < groups - 1)) | ((row >= rows + HALO) & (g > 0))
    lane_ok = (
        (lane < cols)
        | ((lane < cols + HALO) & (t < tiles - 1))
        | ((lane >= cols + LANES - HALO) & (t > 0))
    )
    return row_ok & lane_ok


def unpack_lanes(got_ref, line, rows):
    step = LANES // HALO
    shape = (step, LANES)
    index = row_iota(shape) * HALO + lax.rem(lane_iota(shape), HALO)
    parts = []
    for k in range(rows // step):
        piece = jnp.broadcast_to(got_ref[pl.ds(line + k, 1), :], shape)
        parts.append(gather_lanes(piece, index))
    return jnp.concatenate(parts, axis=0)


def smooth_kernel(
    grid, width, got_ref, rhs_ref, diag_ref, below_ref, above_ref,
    rhs_out, diag_out, weight_out, smooth_out, coarse_out,
):
    groups, tiles = grid
    g, t = lax.axis_index("grp"), lax.axis_index("tile")
    rows, cols = rhs_ref.shape
    up, down = jnp.maximum(g - 1, 0), jnp.minimum(g + 1, groups - 1)
    left, right = jnp.maximum(t - 1, 0), jnp.minimum(t + 1, tiles - 1)
    inside = inside_mask(grid, rows, cols)
    at = 0
    for ref, out, edge in ((rhs_ref, rhs_out, 0), (diag_ref, diag_out, HALO)):
        out[:rows, :cols] = ref[...]
        out[rows : rows + HALO, :cols] = below_ref[edge : edge + HALO, :]
        out[rows + HALO :, :cols] = above_ref[edge : edge + HALO, :]
        sides = []
        for column in (right, left):
            mid = unpack_lanes(got_ref, (g * tiles + column) * width + at, rows)
            low = unpack_lanes(got_ref, (down * tiles + column) * width + at, rows)[:HALO]
            top = unpack_lanes(got_ref, (up * tiles + column) * width + at, rows)[rows - HALO :]
            sides.append(jnp.concatenate([mid, low, top], axis=0))
        lane = lane_iota(sides[0].shape)
        side = jnp.where(lane < HALO, sides[0], 0.0)
        side = jnp.where(lane >= LANES - HALO, sides[1], side)
        out[:, cols:] = side
        at += rows * HALO // LANES
    rhs = jnp.where(inside, rhs_out[...], 0.0)
    diag = jnp.where(inside, diag_out[...], 0.0)
    rhs_out[...] = rhs
    diag_out[...] = diag
    weight = jnp.where(inside, OMEGA / (6.0 + diag), 0.0)
    weight_out[...] = weight
    smooth = weight * rhs
    for _ in range(SWEEPS - 1):
        smooth = (1.0 - OMEGA) * smooth + weight * (rhs + neighbour_sum(smooth))
    smooth_out[...] = smooth
    left_over = (rhs - (6.0 + diag) * smooth + neighbour_sum(smooth))[:rows, :cols]
    coarse = block_means([left_over])
    coarse_out[...] = jnp.broadcast_to(coarse, (SUB, LANES))


def spread_kernel(keep_ref, came_ref, coarse_ref, slots_ref):
    high = keep_ref.shape[0]
    width = high + 1
    half = keep_ref[...] + came_ref[...]
    for device in range(slots_ref.shape[0] // width):
        slots_ref[device * width : device * width + high, :] = half
        slots_ref[device * width + high : (device + 1) * width, :] = coarse_ref[:1, :]


def coarse_operator(value, mean, grid, blocks):
    groups, tiles = grid
    block_rows, per_row = blocks
    here = block_rows * per_row
    shape = value.shape
    lane, row = lane_iota(shape), row_iota(shape)
    device = row * (LANES // here) + lane // here
    a = lax.rem(lane, here) // per_row
    b = lax.rem(lane, per_row)
    tile, group = lax.rem(device, tiles), device // tiles
    per_line = tiles * here // LANES

    def to_right(x):
        near = shift(x, 1, 1)
        far = shift(x, here - per_row + 1, 1)
        far = jnp.where(lane < here, shift(far, 1, 0), far)
        return jnp.where(b > 0, near, jnp.where(tile > 0, far, 0.0))

    def to_left(x):
        near = shift(x, -1, 1)
        far = shift(x, -(here - per_row + 1), 1)
        far = jnp.where(lane >= LANES - here, shift(far, -1, 0), far)
        return jnp.where(b < per_row - 1, near, jnp.where(tile < tiles - 1, far, 0.0))

    def to_below(x):
        near = shift(x, per_row, 1)
        far = shift(shift(x, -(here - per_row), 1), per_line, 0)
        return jnp.where(a > 0, near, jnp.where(group > 0, far, 0.0))

    def to_above(x):
        near = shift(x, -per_row, 1)
        far = shift(shift(x, here - per_row, 1), -per_line, 0)
        return jnp.where(a < block_rows - 1, near, jnp.where(group < groups - 1, far, 0.0))

    above, below = to_below(value), to_above(value)
    sides = above + below + to_right(value) + to_left(value)
    corners = to_left(above) + to_right(below)
    edge = 2.0 * FAC - 1.0
    return mean * value + (edge * (4.0 * value - sides) + (2.0 * value - corners)) * (
        1.0 / (FAC * FAC)
    )


def second_kernel(grid, blocks, got_ref, mean_ref, factor_ref, value_ref, slots_ref):
    groups, tiles = grid
    high = factor_ref.shape[1] // LANES // 2
    width = high + 1
    for side in range(2):
        total = None
        for g in range(side, groups, 2):
            for device in range(g * tiles, (g + 1) * tiles):
                part = got_ref[device * width : device * width + high, :]
                total = part if total is None else total + part
        value_ref[side * high : (side + 1) * high, :] = total
    rest = interleave(*pairs(got_ref, high, width))
    coarse = rest - MIX * coarse_operator(value_ref[...], mean_ref[...], grid, blocks)
    terms = two_products(coarse, factor_ref)
    for m, term in enumerate(terms):
        slots_ref[2 * m : 2 * m + 1, :] = term
        slots_ref[2 * m + 1 : 2 * m + 2, :] = shift(term, LANES // 2, 1)


def prolong_line(line, first, shape):
    index = jnp.broadcast_to(first + lane_iota(shape) // FAC, shape)
    return gather_lanes(jnp.broadcast_to(line, shape), index)


def last_kernel(
    grid, got_ref, value_ref, rhs_ref, diag_ref, weight_ref, smooth_ref, out_ref, field_ref
):
    groups, tiles = grid
    g, t = lax.axis_index("grp"), lax.axis_index("tile")
    rows, cols = out_ref.shape
    block_rows, per_row = rows // FAC, cols // FAC
    here = block_rows * per_row
    inside = inside_mask(grid, rows, cols)
    up, down = jnp.maximum(g - 1, 0), jnp.minimum(g + 1, groups - 1)
    left, right = jnp.maximum(t - 1, 0), jnp.minimum(t + 1, tiles - 1)

    def line_of(device):
        return value_ref[pl.ds(device * here // LANES, 1), :], lax.rem(device * here, LANES)

    bands = [(a * FAC, FAC, g, a) for a in range(block_rows)]
    bands += [(rows, HALO, down, 0), (rows + HALO, HALO, up, block_rows - 1)]
    for start, height, group, a in bands:
        shape = (SUB, LANES)
        line, at = line_of(group * tiles + t)
        parts = [
            prolong_line(line, at + a * per_row + q * (LANES // FAC), shape)
            for q in range(cols // LANES)
        ]
        line, at = line_of(group * tiles + right)
        beside = gather_lanes(
            jnp.broadcast_to(line, shape), jnp.full(shape, at + a * per_row, jnp.int32)
        )
        line, at = line_of(group * tiles + left)
        other = gather_lanes(
            jnp.broadcast_to(line, shape),
            jnp.full(shape, at + (a + 1) * per_row - 1, jnp.int32),
        )
        parts.append(jnp.where(lane_iota(shape) < LANES // 2, beside, other))
        for low in range(start, start + height, SUB):
            for q, part in enumerate(parts):
                field_ref[low : low + SUB, q * LANES : (q + 1) * LANES] = part
    field = jnp.where(inside, smooth_ref[...] + MIX * field_ref[...], 0.0)
    rhs = rhs_ref[...]
    weight = weight_ref[...]
    rest = rhs - (6.0 + diag_ref[...]) * field + neighbour_sum(field)
    smooth = weight * rest
    for _ in range(SWEEPS - 1):
        smooth = (1.0 - OMEGA) * smooth + weight * (rest + neighbour_sum(smooth))
    base = field[:rows, :cols] + smooth[:rows, :cols]
    line = MIX * jnp.sum(got_ref[...], axis=0, keepdims=True)
    for a in range(rows // FAC):
        for q in range(cols // LANES):
            part = prolong_line(line, a * per_row + q * (LANES // FAC), (SUB, LANES))
            for low in range(a * FAC, (a + 1) * FAC, SUB):
                where = (slice(low, low + SUB), slice(q * LANES, (q + 1) * LANES))
                out_ref[where] = base[where] + part


def shards(right_side, diagonal, inverse_factor):
    groups, tiles = lax.axis_size("grp"), lax.axis_size("tile")
    grid = (groups, tiles)
    count = groups * tiles
    rows, cols = right_side.shape
    points = inverse_factor.shape[1]
    high = points // LANES
    blocks = (rows // FAC, cols // FAC)
    everyone = ("grp", "tile")
    swap = [(i, i ^ 1) for i in range(groups)]
    g = lax.axis_index("grp")

    def exchange(slots):
        lines = slots.shape[0] // count
        got = lax.all_to_all(slots.reshape(count, lines * LANES), everyone, 0, 0, tiled=True)
        return got.reshape(count * lines, LANES)

    width = 2 * rows * HALO // LANES + 1
    edge = (2 * HALO, cols)
    shapes = [(count * width, LANES), (rows, cols), (rows, cols), inverse_factor.shape]
    shapes += [edge] * (2 if groups > 2 else 1)
    slots, right_side, diagonal, inverse_factor, *edges = pl.pallas_call(
        functools.partial(start_kernel, grid),
        out_shape=[jax.ShapeDtypeStruct(s, jnp.float32) for s in shapes],
        in_specs=[pl.BlockSpec(memory_space=pltpu.HBM)] * 3,
        out_specs=[VMEM] * len(shapes),
        scratch_shapes=[pltpu.SemaphoreType.DMA((3,))],
        compiler_params=pltpu.CompilerParams(vmem_limit_bytes=LIMIT),
    )(
        *[
            pltpu.with_memory_space_constraint(x, pltpu.HBM)
            for x in (right_side, diagonal, inverse_factor)
        ]
    )
    got = exchange(slots)
    got, edges = lax.optimization_barrier((got, edges))
    near = lax.ppermute(edges[0], "grp", swap)
    if groups > 2:
        across = [(i, i + 1) for i in range(1, groups - 1, 2)]
        across += [(j, i) for i, j in across]
        far = lax.ppermute(edges[1], "grp", across)
        below = jnp.where(g % 2 == 0, near, far)
        above = jnp.where(g % 2 == 0, far, near)
    else:
        below, above = near, near

    half = (high // 2, LANES)
    keep, send, mean = call(
        functools.partial(first_kernel, width), [half, half, (high, LANES)], 2
    )(got, inverse_factor)
    came = lax.ppermute(send, "grp", swap)
    wide = (rows + 2 * HALO, cols + LANES)
    rhs, diag, weight, smooth, coarse = call(
        functools.partial(smooth_kernel, grid, width), [wide] * 4 + [(SUB, LANES)], 5
    )(got, right_side, diagonal, below, above)
    (slots,) = call(spread_kernel, [(count * (high // 2 + 1), LANES)], 3)(keep, came, coarse)
    got = exchange(slots)

    value, slots = call(
        functools.partial(second_kernel, grid, blocks), [(high, LANES), (count, LANES)], 3
    )(got, mean, inverse_factor)
    got = exchange(slots)
    (field,) = call(
        functools.partial(last_kernel, grid), [(rows, cols)], 6, [wide]
    )(got, value, rhs, diag, weight, smooth)
    return field


def solution(mesh):
    placed = (P("grp", "tile"), P("grp", "tile"), P(("grp", "tile"), None))
    return jax.shard_map(
        shards, mesh=mesh, in_specs=placed, out_specs=P("grp", "tile"), check_vma=False
    )
```

```python
import functools

import jax
import jax.numpy as jnp
from jax import lax
from jax.experimental import pallas as pl
from jax.experimental.pallas import tpu as pltpu
from jax.sharding import PartitionSpec as P


FAC = 16
SWEEPS = 4
OMEGA = 0.8
MIX = 0.5
LANES = 128
SUB = 8
HALO = 8

VMEM = pl.BlockSpec(memory_space=pltpu.VMEM)


def limit(points):
    return 4 * 1024 * 1024 + 2048 * points


def call(points, body, shapes, count, scratch=()):
    return pl.pallas_call(
        body,
        out_shape=[jax.ShapeDtypeStruct(s, jnp.float32) for s in shapes],
        in_specs=[VMEM] * count,
        out_specs=[VMEM] * len(shapes),
        scratch_shapes=[pltpu.VMEM(s, jnp.float32) for s in scratch],
        compiler_params=pltpu.CompilerParams(vmem_limit_bytes=limit(points)),
    )


def lane_iota(shape):
    return lax.broadcasted_iota(jnp.int32, shape, len(shape) - 1)


def row_iota(shape):
    return lax.broadcasted_iota(jnp.int32, shape, 0)


def shift(x, by, axis):
    return pltpu.roll(x, by % x.shape[axis], axis)


def neighbour_sum(x):
    above, below = shift(x, 1, 0), shift(x, -1, 0)
    return above + below + shift(x + above, -1, 1) + shift(x + below, 1, 1)


def gather_lanes(x, index):
    return jnp.take_along_axis(x, index, axis=1)


def block_means(arrays):
    rows, cols = arrays[0].shape
    per_row = cols // FAC
    sums = [
        jnp.sum(x[a * FAC : (a + 1) * FAC], axis=0, keepdims=True)
        for x in arrays
        for a in range(rows // FAC)
    ]
    used = len(sums)
    high = jnp.concatenate(sums, axis=0)
    parts = []
    for _ in range(3):
        part = high.astype(jnp.bfloat16)
        parts.append(part.astype(jnp.float32))
        high = high - parts[-1]
    fill = -len(parts) * used % (2 * SUB)
    tall = jnp.concatenate(parts + [jnp.zeros((fill, cols), jnp.float32)], axis=0)
    pick = (
        lax.broadcasted_iota(jnp.int32, (cols, LANES), 0) // FAC
        == lax.rem(lane_iota((cols, LANES)), per_row)
    )
    line = jnp.dot(
        tall.astype(jnp.bfloat16),
        pick.astype(jnp.bfloat16),
        preferred_element_type=jnp.float32,
    )
    mine = lax.rem(row_iota(line.shape), used) == lax.rem(lane_iota(line.shape) // per_row, used)
    line = jnp.where(mine, line, 0.0)
    return jnp.sum(line, axis=0, keepdims=True) * (1.0 / (FAC * FAC))


def pack_lanes(strip, first):
    step = LANES // HALO
    parts = []
    for at in range(0, strip.shape[0], step):
        piece = strip[at : at + step]
        lane, row = lane_iota(piece.shape), row_iota(piece.shape)
        piece = gather_lanes(piece, first + lax.rem(lane, HALO))
        piece = jnp.where(lane // HALO == row, piece, 0.0)
        parts.append(jnp.sum(piece, axis=0, keepdims=True))
    return parts


def start_kernel(
    grid, rhs_in, diag_in, factor_in, slots_ref, rhs_ref, diag_ref, mine_ref, *rest
):
    edge_refs, sems = rest[:-1], rest[-1]
    here = factor_in.shape[0]
    factor_ref = mine_ref.at[:here, :]
    loads = [
        pltpu.make_async_copy(source, target, sems.at[k])
        for k, (source, target) in enumerate(
            ((rhs_in, rhs_ref), (diag_in, diag_ref), (factor_in, factor_ref))
        )
    ]
    for load in loads:
        load.start()
    groups, tiles = grid
    g, t = lax.axis_index("grp"), lax.axis_index("tile")
    rows, cols = rhs_ref.shape
    count = groups * tiles
    even = lax.rem(g, 2) == 0
    loads[0].wait()
    loads[1].wait()
    for at, ref in ((0, rhs_ref), (cols, diag_ref)):
        first, last = ref[:HALO, :], ref[rows - HALO :, :]
        mine_ref[here:, at : at + cols] = jnp.where(even, last, first)
        for edge_ref in edge_refs:
            edge_ref[:, at : at + cols] = jnp.where(even, first, last)
    coarse = block_means([rhs_ref[...], diag_ref[...]])
    to_left = lax.rem(row_iota((count, LANES)), tiles) < t
    lines = []
    for ref in (rhs_ref, diag_ref):
        left = pack_lanes(ref[:, :LANES], 0)
        right = pack_lanes(ref[:, cols - LANES :], LANES - HALO)
        lines += [jnp.where(to_left, one, two) for one, two in zip(left, right)]
    lines.append(jnp.broadcast_to(coarse, (count, LANES)))
    for k, line in enumerate(lines):
        slots_ref[pl.ds(k, count, stride=len(lines)), :] = line
    loads[2].wait()


def products(vector, factor_ref, here):
    total = None
    for m in range(vector.shape[0]):
        term = factor_ref[:here, m * LANES : (m + 1) * LANES] * vector[m : m + 1, :]
        total = term if total is None else total + term
    return jnp.sum(total, axis=1, keepdims=True)


def interleave(even, odd):
    return jnp.where(lane_iota(even.shape) < LANES // 2, even, odd)


def pairs(ref, line, width):
    count = ref.shape[0] // width
    return [
        ref[pl.ds(line + side * width, count // 2, stride=2 * width), :] for side in range(2)
    ]


def inside_mask(grid, rows, cols):
    groups, tiles = grid
    g, t = lax.axis_index("grp"), lax.axis_index("tile")
    shape = (rows + 2 * HALO, cols + LANES)
    row, lane = row_iota(shape), lane_iota(shape)
    row_ok = (row < rows) | ((row < rows + HALO) & (g < groups - 1)) | ((row >= rows + HALO) & (g > 0))
    lane_ok = (
        (lane < cols)
        | ((lane < cols + HALO) & (t < tiles - 1))
        | ((lane >= cols + LANES - HALO) & (t > 0))
    )
    return row_ok & lane_ok


def unpack_lanes(got_ref, line, rows):
    step = LANES // HALO
    shape = (step, LANES)
    index = row_iota(shape) * HALO + lax.rem(lane_iota(shape), HALO)
    parts = []
    for k in range(rows // step):
        piece = jnp.broadcast_to(got_ref[pl.ds(line + k, 1), :], shape)
        parts.append(gather_lanes(piece, index))
    return jnp.concatenate(parts, axis=0)


def middle_kernel(
    grid, width, got_ref, rhs_ref, diag_ref, mine_ref, theirs_ref, *refs
):
    far_refs, (rhs_out, diag_out, weight_out, smooth_out, mean_ref, slots_ref, half_ref) = (
        refs[:-7],
        refs[-7:],
    )
    groups, tiles = grid
    g, t = lax.axis_index("grp"), lax.axis_index("tile")
    rows, cols = rhs_ref.shape
    here = mine_ref.shape[0] - HALO
    high = half_ref.shape[0]
    even, odd = pairs(got_ref, width - 1, width)
    mean_ref[...] = interleave(shift(even, LANES // 2, 1), odd)
    vector = interleave(even, shift(odd, LANES // 2, 1))
    inner = products(vector, mine_ref, here)
    other = products(vector, theirs_ref, here)
    start = lax.rem(g, 2) * (high * LANES)
    for m in range(high):
        place = pl.ds(pl.multiple_of(start + m * LANES, LANES), LANES)
        term = mine_ref[:here, place] * inner + theirs_ref[:here, place] * other
        half_ref[m : m + 1, :] = jnp.sum(term, axis=0, keepdims=True)
    near_ref = theirs_ref.at[here:, :]
    if groups > 2:
        near, far = near_ref[:, : 2 * cols], far_refs[0][...]
        is_even = lax.rem(g, 2) == 0
        below, above = jnp.where(is_even, near, far), jnp.where(is_even, far, near)
    else:
        below = above = near_ref[:, : 2 * cols]
    up, down = jnp.maximum(g - 1, 0), jnp.minimum(g + 1, groups - 1)
    left, right = jnp.maximum(t - 1, 0), jnp.minimum(t + 1, tiles - 1)
    inside = inside_mask(grid, rows, cols)
    at = 0
    for ref, out, edge in ((rhs_ref, rhs_out, 0), (diag_ref, diag_out, cols)):
        out[:rows, :cols] = ref[...]
        out[rows : rows + HALO, :cols] = below[:, edge : edge + cols]
        out[rows + HALO :, :cols] = above[:, edge : edge + cols]
        sides = []
        for column in (right, left):
            mid = unpack_lanes(got_ref, (g * tiles + column) * width + at, rows)
            low = unpack_lanes(got_ref, (down * tiles + column) * width + at, rows)[:HALO]
            top = unpack_lanes(got_ref, (up * tiles + column) * width + at, rows)[rows - HALO :]
            sides.append(jnp.concatenate([mid, low, top], axis=0))
        lane = lane_iota(sides[0].shape)
        side = jnp.where(lane < HALO, sides[0], 0.0)
        side = jnp.where(lane >= LANES - HALO, sides[1], side)
        out[:, cols:] = side
        at += rows * HALO // LANES
    rhs = jnp.where(inside, rhs_out[...], 0.0)
    diag = jnp.where(inside, diag_out[...], 0.0)
    rhs_out[...] = rhs
    diag_out[...] = diag
    weight = jnp.where(inside, OMEGA / (6.0 + diag), 0.0)
    weight_out[...] = weight
    smooth = weight * rhs
    for _ in range(SWEEPS - 1):
        smooth = (1.0 - OMEGA) * smooth + weight * (rhs + neighbour_sum(smooth))
    smooth_out[...] = smooth
    left_over = (rhs - (6.0 + diag) * smooth + neighbour_sum(smooth))[:rows, :cols]
    coarse = block_means([left_over])
    half = half_ref[...]
    for device in range(groups * tiles):
        slots_ref[device * (high + 1) : device * (high + 1) + high, :] = half
        slots_ref[device * (high + 1) + high : (device + 1) * (high + 1), :] = coarse


def coarse_operator(value, mean, grid, blocks):
    groups, tiles = grid
    block_rows, per_row = blocks
    here = block_rows * per_row
    shape = value.shape
    lane, row = lane_iota(shape), row_iota(shape)
    device = row * (LANES // here) + lane // here
    a = lax.rem(lane, here) // per_row
    b = lax.rem(lane, per_row)
    tile, group = lax.rem(device, tiles), device // tiles
    per_line = tiles * here // LANES

    def to_right(x):
        near = shift(x, 1, 1)
        far = shift(x, here - per_row + 1, 1)
        far = jnp.where(lane < here, shift(far, 1, 0), far)
        return jnp.where(b > 0, near, jnp.where(tile > 0, far, 0.0))

    def to_left(x):
        near = shift(x, -1, 1)
        far = shift(x, -(here - per_row + 1), 1)
        far = jnp.where(lane >= LANES - here, shift(far, -1, 0), far)
        return jnp.where(b < per_row - 1, near, jnp.where(tile < tiles - 1, far, 0.0))

    def to_below(x):
        near = shift(x, per_row, 1)
        far = shift(shift(x, -(here - per_row), 1), per_line, 0)
        return jnp.where(a > 0, near, jnp.where(group > 0, far, 0.0))

    def to_above(x):
        near = shift(x, -per_row, 1)
        far = shift(shift(x, here - per_row, 1), -per_line, 0)
        return jnp.where(a < block_rows - 1, near, jnp.where(group < groups - 1, far, 0.0))

    above, below = to_below(value), to_above(value)
    sides = above + below + to_right(value) + to_left(value)
    corners = to_left(above) + to_right(below)
    edge = 2.0 * FAC - 1.0
    return mean * value + (edge * (4.0 * value - sides) + (2.0 * value - corners)) * (
        1.0 / (FAC * FAC)
    )


def second_kernel(grid, blocks, got_ref, mean_ref, mine_ref, value_ref, slots_ref):
    groups, tiles = grid
    here = mine_ref.shape[0] - HALO
    high = mine_ref.shape[1] // LANES // 2
    width = high + 1
    for side in range(2):
        total = None
        for g in range(side, groups, 2):
            for device in range(g * tiles, (g + 1) * tiles):
                part = got_ref[device * width : device * width + high, :]
                total = part if total is None else total + part
        value_ref[side * high : (side + 1) * high, :] = total
    rest = interleave(*pairs(got_ref, high, width))
    coarse = rest - MIX * coarse_operator(value_ref[...], mean_ref[...], grid, blocks)
    inner = products(coarse, mine_ref, here)
    for m in range(2 * high):
        term = mine_ref[:here, m * LANES : (m + 1) * LANES] * inner
        term = jnp.sum(term, axis=0, keepdims=True)
        slots_ref[2 * m : 2 * m + 1, :] = term
        slots_ref[2 * m + 1 : 2 * m + 2, :] = shift(term, LANES // 2, 1)


def prolong_line(line, first, shape):
    index = jnp.broadcast_to(first + lane_iota(shape) // FAC, shape)
    return gather_lanes(jnp.broadcast_to(line, shape), index)


def last_kernel(
    grid, got_ref, value_ref, rhs_ref, diag_ref, weight_ref, smooth_ref, out_ref, field_ref
):
    groups, tiles = grid
    g, t = lax.axis_index("grp"), lax.axis_index("tile")
    rows, cols = out_ref.shape
    block_rows, per_row = rows // FAC, cols // FAC
    here = block_rows * per_row
    inside = inside_mask(grid, rows, cols)
    up, down = jnp.maximum(g - 1, 0), jnp.minimum(g + 1, groups - 1)
    left, right = jnp.maximum(t - 1, 0), jnp.minimum(t + 1, tiles - 1)

    def line_of(device):
        return value_ref[pl.ds(device * here // LANES, 1), :], lax.rem(device * here, LANES)

    bands = [(a * FAC, FAC, g, a) for a in range(block_rows)]
    bands += [(rows, HALO, down, 0), (rows + HALO, HALO, up, block_rows - 1)]
    for start, height, group, a in bands:
        shape = (SUB, LANES)
        line, at = line_of(group * tiles + t)
        parts = [
            prolong_line(line, at + a * per_row + q * (LANES // FAC), shape)
            for q in range(cols // LANES)
        ]
        line, at = line_of(group * tiles + right)
        beside = gather_lanes(
            jnp.broadcast_to(line, shape), jnp.full(shape, at + a * per_row, jnp.int32)
        )
        line, at = line_of(group * tiles + left)
        other = gather_lanes(
            jnp.broadcast_to(line, shape),
            jnp.full(shape, at + (a + 1) * per_row - 1, jnp.int32),
        )
        parts.append(jnp.where(lane_iota(shape) < LANES // 2, beside, other))
        for low in range(start, start + height, SUB):
            for q, part in enumerate(parts):
                field_ref[low : low + SUB, q * LANES : (q + 1) * LANES] = part
    field = jnp.where(inside, smooth_ref[...] + MIX * field_ref[...], 0.0)
    rhs = rhs_ref[...]
    weight = weight_ref[...]
    rest = rhs - (6.0 + diag_ref[...]) * field + neighbour_sum(field)
    smooth = weight * rest
    for _ in range(SWEEPS - 1):
        smooth = (1.0 - OMEGA) * smooth + weight * (rest + neighbour_sum(smooth))
    base = field[:rows, :cols] + smooth[:rows, :cols]
    line = MIX * jnp.sum(got_ref[...], axis=0, keepdims=True)
    for a in range(rows // FAC):
        for q in range(cols // LANES):
            part = prolong_line(line, a * per_row + q * (LANES // FAC), (SUB, LANES))
            for low in range(a * FAC, (a + 1) * FAC, SUB):
                where = (slice(low, low + SUB), slice(q * LANES, (q + 1) * LANES))
                out_ref[where] = base[where] + part


def shards(right_side, diagonal, inverse_factor):
    groups, tiles = lax.axis_size("grp"), lax.axis_size("tile")
    grid = (groups, tiles)
    count = groups * tiles
    rows, cols = right_side.shape
    points = inverse_factor.shape[1]
    high = points // LANES
    blocks = (rows // FAC, cols // FAC)
    everyone = ("grp", "tile")

    def exchange(slots):
        lines = slots.shape[0] // count
        got = lax.all_to_all(slots.reshape(count, lines * LANES), everyone, 0, 0, tiled=True)
        return got.reshape(count * lines, LANES)

    width = 2 * rows * HALO // LANES + 1
    here = inverse_factor.shape[0]
    shapes = [(count * width, LANES), (rows, cols), (rows, cols), (here + HALO, points)]
    shapes += [(HALO, 2 * cols)] if groups > 2 else []
    slots, right_side, diagonal, mine, *edges = pl.pallas_call(
        functools.partial(start_kernel, grid),
        out_shape=[jax.ShapeDtypeStruct(s, jnp.float32) for s in shapes],
        in_specs=[pl.BlockSpec(memory_space=pltpu.HBM)] * 3,
        out_specs=[VMEM] * len(shapes),
        scratch_shapes=[pltpu.SemaphoreType.DMA((3,))],
        compiler_params=pltpu.CompilerParams(vmem_limit_bytes=limit(points)),
    )(
        *[
            pltpu.with_memory_space_constraint(x, pltpu.HBM)
            for x in (right_side, diagonal, inverse_factor)
        ]
    )
    theirs = lax.ppermute(mine, "grp", [(i, i ^ 1) for i in range(groups)])
    far = []
    if groups > 2:
        across = [(i, i + 1) for i in range(1, groups - 1, 2)]
        across += [(j, i) for i, j in across]
        far = [lax.ppermute(edges[0], "grp", across)]
    got = exchange(slots)

    wide = (rows + 2 * HALO, cols + LANES)
    rhs, diag, weight, smooth, mean, slots = call(
        points,
        functools.partial(middle_kernel, grid, width),
        [wide] * 4 + [(high, LANES), (count * (high // 2 + 1), LANES)],
        5 + len(far),
        [(high // 2, LANES)],
    )(got, right_side, diagonal, mine, theirs, *far)
    got = exchange(slots)

    value, slots = call(
        points,
        functools.partial(second_kernel, grid, blocks),
        [(high, LANES), (count, LANES)],
        3,
    )(got, mean, mine)
    got = exchange(slots)
    (field,) = call(
        points, functools.partial(last_kernel, grid), [(rows, cols)], 6, [wide]
    )(got, value, rhs, diag, weight, smooth)
    return field


def solution(mesh):
    placed = (P("grp", "tile"), P("grp", "tile"), P(("grp", "tile"), None))

    return jax.shard_map(
        shards, mesh=mesh, in_specs=placed, out_specs=P("grp", "tile"), check_vma=False
    )
```

```python
import functools

import jax
import jax.numpy as jnp
from jax import lax
from jax.experimental import pallas as pl
from jax.experimental.pallas import tpu as pltpu
from jax.sharding import PartitionSpec as P


FAC = 16
SWEEPS = 4
OMEGA = 0.8
MIX = 0.5
LANES = 128
SUB = 8
HALO = 8

VMEM = pl.BlockSpec(memory_space=pltpu.VMEM)


def limit(points):
    return 4 * 1024 * 1024 + 2048 * points


def call(points, body, shapes, count, scratch=()):
    return pl.pallas_call(
        body,
        out_shape=[jax.ShapeDtypeStruct(s, jnp.float32) for s in shapes],
        in_specs=[VMEM] * count,
        out_specs=[VMEM] * len(shapes),
        scratch_shapes=[pltpu.VMEM(s, jnp.float32) for s in scratch],
        compiler_params=pltpu.CompilerParams(vmem_limit_bytes=limit(points)),
    )


def lane_iota(shape):
    return lax.broadcasted_iota(jnp.int32, shape, len(shape) - 1)


def row_iota(shape):
    return lax.broadcasted_iota(jnp.int32, shape, 0)


def shift(x, by, axis):
    return pltpu.roll(x, by % x.shape[axis], axis)


def neighbour_sum(x):
    above, below = shift(x, 1, 0), shift(x, -1, 0)
    return above + below + shift(x + above, -1, 1) + shift(x + below, 1, 1)


def gather_lanes(x, index):
    return jnp.take_along_axis(x, index, axis=1)


def block_means(arrays):
    rows, cols = arrays[0].shape
    per_row = cols // FAC
    sums = [
        jnp.sum(x[a * FAC : (a + 1) * FAC], axis=0, keepdims=True)
        for x in arrays
        for a in range(rows // FAC)
    ]
    used = len(sums)
    high = jnp.concatenate(sums, axis=0)
    parts = []
    for _ in range(3):
        part = high.astype(jnp.bfloat16)
        parts.append(part.astype(jnp.float32))
        high = high - parts[-1]
    fill = -len(parts) * used % (2 * SUB)
    tall = jnp.concatenate(parts + [jnp.zeros((fill, cols), jnp.float32)], axis=0)
    pick = (
        lax.broadcasted_iota(jnp.int32, (cols, LANES), 0) // FAC
        == lax.rem(lane_iota((cols, LANES)), per_row)
    )
    line = jnp.dot(
        tall.astype(jnp.bfloat16),
        pick.astype(jnp.bfloat16),
        preferred_element_type=jnp.float32,
    )
    mine = lax.rem(row_iota(line.shape), used) == lax.rem(lane_iota(line.shape) // per_row, used)
    line = jnp.where(mine, line, 0.0)
    return jnp.sum(line, axis=0, keepdims=True) * (1.0 / (FAC * FAC))


def pack_lanes(strip, first):
    step = LANES // HALO
    parts = []
    for at in range(0, strip.shape[0], step):
        piece = strip[at : at + step]
        lane, row = lane_iota(piece.shape), row_iota(piece.shape)
        piece = gather_lanes(piece, first + lax.rem(lane, HALO))
        piece = jnp.where(lane // HALO == row, piece, 0.0)
        parts.append(jnp.sum(piece, axis=0, keepdims=True))
    return parts


def start_kernel(
    grid, rhs_in, diag_in, factor_in, slots_ref, rhs_ref, diag_ref, mine_ref, *rest
):
    edge_refs, sems = rest[:-1], rest[-1]
    here = factor_in.shape[0]
    factor_ref = mine_ref.at[:here, :]
    loads = [
        pltpu.make_async_copy(source, target, sems.at[k])
        for k, (source, target) in enumerate(
            ((rhs_in, rhs_ref), (diag_in, diag_ref), (factor_in, factor_ref))
        )
    ]
    for load in loads:
        load.start()
    groups, tiles = grid
    g, t = lax.axis_index("grp"), lax.axis_index("tile")
    rows, cols = rhs_ref.shape
    count = groups * tiles
    even = lax.rem(g, 2) == 0
    loads[0].wait()
    loads[1].wait()
    for at, ref in ((0, rhs_ref), (cols, diag_ref)):
        first, last = ref[:HALO, :], ref[rows - HALO :, :]
        mine_ref[here:, at : at + cols] = jnp.where(even, last, first)
        for edge_ref in edge_refs:
            edge_ref[:, at : at + cols] = jnp.where(even, first, last)
    coarse = block_means([rhs_ref[...], diag_ref[...]])
    to_left = lax.rem(row_iota((count, LANES)), tiles) < t
    lines = []
    for ref in (rhs_ref, diag_ref):
        left = pack_lanes(ref[:, :LANES], 0)
        right = pack_lanes(ref[:, cols - LANES :], LANES - HALO)
        lines += [jnp.where(to_left, one, two) for one, two in zip(left, right)]
    lines.append(jnp.broadcast_to(coarse, (count, LANES)))
    for k, line in enumerate(lines):
        slots_ref[pl.ds(k, count, stride=len(lines)), :] = line
    loads[2].wait()


def products(vector, factor_ref, here):
    total = None
    for m in range(vector.shape[0]):
        term = factor_ref[:here, m * LANES : (m + 1) * LANES] * vector[m : m + 1, :]
        total = term if total is None else total + term
    return jnp.sum(total, axis=1, keepdims=True)


def interleave(even, odd):
    return jnp.where(lane_iota(even.shape) < LANES // 2, even, odd)


def pairs(ref, line, width):
    count = ref.shape[0] // width
    return [
        ref[pl.ds(line + side * width, count // 2, stride=2 * width), :] for side in range(2)
    ]


def inside_mask(grid, rows, cols):
    groups, tiles = grid
    g, t = lax.axis_index("grp"), lax.axis_index("tile")
    shape = (rows + 2 * HALO, cols + LANES)
    row, lane = row_iota(shape), lane_iota(shape)
    row_ok = (row < rows) | ((row < rows + HALO) & (g < groups - 1)) | ((row >= rows + HALO) & (g > 0))
    lane_ok = (
        (lane < cols)
        | ((lane < cols + HALO) & (t < tiles - 1))
        | ((lane >= cols + LANES - HALO) & (t > 0))
    )
    return row_ok & lane_ok


def unpack_lanes(got_ref, line, rows):
    step = LANES // HALO
    shape = (step, LANES)
    index = row_iota(shape) * HALO + lax.rem(lane_iota(shape), HALO)
    parts = []
    for k in range(rows // step):
        piece = jnp.broadcast_to(got_ref[pl.ds(line + k, 1), :], shape)
        parts.append(gather_lanes(piece, index))
    return jnp.concatenate(parts, axis=0)


def middle_kernel(
    grid, width, got_ref, rhs_ref, diag_ref, mine_ref, theirs_ref, *refs
):
    far_refs, outs = refs[:-8], refs[-8:]
    rhs_out, diag_out, weight_out, smooth_out, term_ref, ring_ref, slots_ref, term_scr = outs
    groups, tiles = grid
    g, t = lax.axis_index("grp"), lax.axis_index("tile")
    rows, cols = rhs_ref.shape
    here = mine_ref.shape[0] - HALO
    even, odd = pairs(got_ref, width - 1, width)
    mean = interleave(shift(even, LANES // 2, 1), odd)
    vector = interleave(even, shift(odd, LANES // 2, 1))
    inner = products(vector, mine_ref, here)
    other = products(vector, theirs_ref, here)
    for m in range(vector.shape[0]):
        place = slice(m * LANES, (m + 1) * LANES)
        term = mine_ref[:here, place] * inner + theirs_ref[:here, place] * other
        term_scr[m : m + 1, :] = jnp.sum(term, axis=0, keepdims=True)
    term = term_scr[...]
    coarse_grid = Coarse(term.shape, grid, (rows // FAC, cols // FAC))
    next_rhs = -MIX * coarse_operator(term, mean, coarse_grid)
    own = lax.rem(coarse_grid.group, 2) == lax.rem(g, 2)
    ends, columns = (jnp.where(own, x, 0.0) for x in around(term, coarse_grid))
    term = jnp.where(own, term, 0.0)
    half_lane = LANES // 2
    for k, x in enumerate((shift(term, half_lane, 1), term)):
        term_ref[k] = x
    ring_ref[0] = interleave(ends, shift(columns, half_lane, 1))
    ring_ref[1] = interleave(shift(ends, half_lane, 1), columns)
    near_ref = theirs_ref.at[here:, :]
    if groups > 2:
        near, far = near_ref[:, : 2 * cols], far_refs[0][...]
        is_even = lax.rem(g, 2) == 0
        below, above = jnp.where(is_even, near, far), jnp.where(is_even, far, near)
    else:
        below = above = near_ref[:, : 2 * cols]
    up, down = jnp.maximum(g - 1, 0), jnp.minimum(g + 1, groups - 1)
    left, right = jnp.maximum(t - 1, 0), jnp.minimum(t + 1, tiles - 1)
    inside = inside_mask(grid, rows, cols)
    at = 0
    for ref, out, edge in ((rhs_ref, rhs_out, 0), (diag_ref, diag_out, cols)):
        out[:rows, :cols] = ref[...]
        out[rows : rows + HALO, :cols] = below[:, edge : edge + cols]
        out[rows + HALO :, :cols] = above[:, edge : edge + cols]
        sides = []
        for column in (right, left):
            mid = unpack_lanes(got_ref, (g * tiles + column) * width + at, rows)
            low = unpack_lanes(got_ref, (down * tiles + column) * width + at, rows)[:HALO]
            top = unpack_lanes(got_ref, (up * tiles + column) * width + at, rows)[rows - HALO :]
            sides.append(jnp.concatenate([mid, low, top], axis=0))
        lane = lane_iota(sides[0].shape)
        side = jnp.where(lane < HALO, sides[0], 0.0)
        side = jnp.where(lane >= LANES - HALO, sides[1], side)
        out[:, cols:] = side
        at += rows * HALO // LANES
    rhs = jnp.where(inside, rhs_out[...], 0.0)
    diag = jnp.where(inside, diag_out[...], 0.0)
    rhs_out[...] = rhs
    diag_out[...] = diag
    weight = jnp.where(inside, OMEGA / (6.0 + diag), 0.0)
    weight_out[...] = weight
    smooth = weight * rhs
    for _ in range(SWEEPS - 1):
        smooth = (1.0 - OMEGA) * smooth + weight * (rhs + neighbour_sum(smooth))
    smooth_out[...] = smooth
    left_over = (rhs - (6.0 + diag) * smooth + neighbour_sum(smooth))[:rows, :cols]
    coarse = block_means([left_over])
    per_group = coarse_grid.per_group
    is_even = lax.rem(g, 2) == 0
    half = jnp.concatenate(
        [
            jnp.where(is_even, next_rhs[k : k + per_group], next_rhs[k + per_group : k + 2 * per_group])
            for k in range(0, groups * per_group, 2 * per_group)
        ],
        axis=0,
    )
    at = (g // 2) * tiles + t
    devices = LANES // here
    mine = row_iota(half.shape) * devices + lane_iota(half.shape) // here == at
    half = half + jnp.where(mine, coarse, 0.0)
    high = half.shape[0]
    for device in range(groups * tiles):
        slots_ref[device * high : (device + 1) * high, :] = half


class Coarse:
    def __init__(self, shape, grid, blocks):
        self.groups, self.tiles = grid
        self.block_rows, self.per_row = blocks
        self.here = self.block_rows * self.per_row
        self.per_group = self.tiles * self.here // LANES
        self.lane = lane_iota(shape)
        device = row_iota(shape) * (LANES // self.here) + self.lane // self.here
        self.a = lax.rem(self.lane, self.here) // self.per_row
        self.b = lax.rem(self.lane, self.per_row)
        self.tile, self.group = lax.rem(device, self.tiles), device // self.tiles

    def left_of(self, x):
        near = shift(x, 1, 1)
        far = shift(x, self.here - self.per_row + 1, 1)
        far = jnp.where(self.lane < self.here, shift(far, 1, 0), far)
        return jnp.where(self.b > 0, near, jnp.where(self.tile > 0, far, 0.0))

    def right_of(self, x):
        near = shift(x, -1, 1)
        far = shift(x, -(self.here - self.per_row + 1), 1)
        far = jnp.where(self.lane >= LANES - self.here, shift(far, -1, 0), far)
        last = self.tile < self.tiles - 1
        return jnp.where(self.b < self.per_row - 1, near, jnp.where(last, far, 0.0))

    def above(self, x):
        near = shift(x, self.per_row, 1)
        far = shift(shift(x, -(self.here - self.per_row), 1), self.per_group, 0)
        return jnp.where(self.a > 0, near, jnp.where(self.group > 0, far, 0.0))

    def below(self, x):
        near = shift(x, -self.per_row, 1)
        far = shift(shift(x, self.here - self.per_row, 1), -self.per_group, 0)
        last = self.group < self.groups - 1
        return jnp.where(self.a < self.block_rows - 1, near, jnp.where(last, far, 0.0))


def coarse_operator(x, mean, coarse):
    above, below = coarse.above(x), coarse.below(x)
    sides = above + below + coarse.left_of(x) + coarse.right_of(x)
    corners = coarse.right_of(above) + coarse.left_of(below)
    edge = 2.0 * FAC - 1.0
    return mean * x + (edge * (4.0 * x - sides) + (2.0 * x - corners)) * (1.0 / (FAC * FAC))


def around(x, coarse):
    ends = jnp.where(coarse.a == 0, coarse.above(x), coarse.below(x))
    last = coarse.per_row - 1

    def sides(y):
        return jnp.where(coarse.b == 0, coarse.left_of(y), coarse.right_of(y))

    own, outer = sides(x), sides(ends)
    columns = jnp.where(coarse.b == 1, shift(outer, 1, 1), own)
    return ends, jnp.where(coarse.b == last - 1, shift(outer, -1, 1), columns)


def second_kernel(grid, per_group, got_ref, mine_ref, term_ref, ring_ref, slots_ref, value_ref):
    groups, tiles = grid
    here = mine_ref.shape[0] - HALO
    lines = mine_ref.shape[1] // LANES
    high = lines // 2
    parts = [None] * groups
    for side in range(2):
        total = None
        for g in range(side, groups, 2):
            for device in range(g * tiles, (g + 1) * tiles):
                part = got_ref[device * high : (device + 1) * high, :]
                total = part if total is None else total + part
        for k in range(groups // 2):
            parts[2 * k + side] = total[k * per_group : (k + 1) * per_group]
    inner = products(jnp.concatenate(parts, axis=0), mine_ref, here)
    for m in range(lines):
        term = mine_ref[:here, m * LANES : (m + 1) * LANES] * inner
        value_ref[m : m + 1, :] = jnp.sum(term, axis=0, keepdims=True)
    value = value_ref[...]
    slots_ref[pl.ds(0, lines, stride=4), :] = interleave(value, term_ref[0])
    slots_ref[pl.ds(1, lines, stride=4), :] = ring_ref[0]
    slots_ref[pl.ds(2, lines, stride=4), :] = interleave(shift(value, LANES // 2, 1), term_ref[1])
    slots_ref[pl.ds(3, lines, stride=4), :] = ring_ref[1]


def prolong_line(line, first, shape):
    index = jnp.broadcast_to(first + lane_iota(shape) // FAC, shape)
    return gather_lanes(jnp.broadcast_to(line, shape), index)


def last_kernel(grid, got_ref, rhs_ref, diag_ref, weight_ref, smooth_ref, out_ref, field_ref):
    rows, cols = out_ref.shape
    block_rows, per_row, per_tile = rows // FAC, cols // FAC, LANES // FAC
    here = block_rows * per_row
    inside = inside_mask(grid, rows, cols)
    shape = (SUB, LANES)
    total = got_ref[:SUB, :]
    for at in range(SUB, got_ref.shape[0], SUB):
        total = total + got_ref[at : at + SUB, :]
    total = total + shift(total, SUB // 2, 0)
    total = total + shift(total, SUB // 4, 0)
    second, ring = total[:1], total[1:2]

    def pick(line, at):
        return gather_lanes(jnp.broadcast_to(line, shape), jnp.full(shape, at, jnp.int32))

    bands = [(a * FAC, FAC, second, here + a * per_row, here + a * per_row) for a in range(block_rows)]
    bands += [(rows, HALO, ring, per_row, here + per_row), (rows + HALO, HALO, ring, 0, here)]
    for start, height, line, at, side in bands:
        parts = [prolong_line(line, at + q * per_tile, shape) for q in range(cols // LANES)]
        step = 0 if start < rows else 1
        beside, other = pick(ring, side + per_row - 1 - step), pick(ring, side + step)
        parts.append(jnp.where(lane_iota(shape) < LANES // 2, beside, other))
        for low in range(start, start + height, SUB):
            for q, part in enumerate(parts):
                field_ref[low : low + SUB, q * LANES : (q + 1) * LANES] = part
    field = jnp.where(inside, smooth_ref[...] + MIX * field_ref[...], 0.0)
    rhs = rhs_ref[...]
    weight = weight_ref[...]
    rest = rhs - (6.0 + diag_ref[...]) * field + neighbour_sum(field)
    smooth = weight * rest
    for _ in range(SWEEPS - 1):
        smooth = (1.0 - OMEGA) * smooth + weight * (rest + neighbour_sum(smooth))
    base = field[:rows, :cols] + smooth[:rows, :cols]
    line = MIX * second
    for a in range(rows // FAC):
        for q in range(cols // LANES):
            part = prolong_line(line, a * per_row + q * (LANES // FAC), (SUB, LANES))
            for low in range(a * FAC, (a + 1) * FAC, SUB):
                where = (slice(low, low + SUB), slice(q * LANES, (q + 1) * LANES))
                out_ref[where] = base[where] + part


def shards(right_side, diagonal, inverse_factor):
    groups, tiles = lax.axis_size("grp"), lax.axis_size("tile")
    grid = (groups, tiles)
    count = groups * tiles
    rows, cols = right_side.shape
    points = inverse_factor.shape[1]
    high = points // LANES
    assert 2 * inverse_factor.shape[0] == LANES and rows == 2 * FAC and groups % 2 == 0
    everyone = ("grp", "tile")

    def exchange(slots):
        lines = slots.shape[0] // count
        got = lax.all_to_all(slots.reshape(count, lines * LANES), everyone, 0, 0, tiled=True)
        return got.reshape(count * lines, LANES)

    width = 2 * rows * HALO // LANES + 1
    here = inverse_factor.shape[0]
    shapes = [(count * width, LANES), (rows, cols), (rows, cols), (here + HALO, points)]
    shapes += [(HALO, 2 * cols)] if groups > 2 else []
    slots, right_side, diagonal, mine, *edges = pl.pallas_call(
        functools.partial(start_kernel, grid),
        out_shape=[jax.ShapeDtypeStruct(s, jnp.float32) for s in shapes],
        in_specs=[pl.BlockSpec(memory_space=pltpu.HBM)] * 3,
        out_specs=[VMEM] * len(shapes),
        scratch_shapes=[pltpu.SemaphoreType.DMA((3,))],
        compiler_params=pltpu.CompilerParams(vmem_limit_bytes=limit(points)),
    )(
        *[
            pltpu.with_memory_space_constraint(x, pltpu.HBM)
            for x in (right_side, diagonal, inverse_factor)
        ]
    )
    theirs = lax.ppermute(mine, "grp", [(i, i ^ 1) for i in range(groups)])
    far = []
    if groups > 2:
        across = [(i, i + 1) for i in range(1, groups - 1, 2)]
        across += [(j, i) for i, j in across]
        far = [lax.ppermute(edges[0], "grp", across)]
    got = exchange(slots)

    wide = (rows + 2 * HALO, cols + LANES)
    rhs, diag, weight, smooth, term, ring, slots = call(
        points,
        functools.partial(middle_kernel, grid, width),
        [wide] * 4 + [(2, high, LANES)] * 2 + [(count * high // 2, LANES)],
        5 + len(far),
        [(high, LANES)],
    )(got, right_side, diagonal, mine, theirs, *far)
    got = exchange(slots)

    (slots,) = call(
        points,
        functools.partial(second_kernel, grid, high // groups),
        [(2 * count, LANES)],
        4,
        [(high, LANES)],
    )(got, mine, term, ring)
    got = exchange(slots)
    (field,) = call(
        points, functools.partial(last_kernel, grid), [(rows, cols)], 5, [wide]
    )(got, rhs, diag, weight, smooth)
    return field


def solution(mesh):
    placed = (P("grp", "tile"), P("grp", "tile"), P(("grp", "tile"), None))

    return jax.shard_map(shards, mesh=mesh, in_specs=placed, out_specs=P("grp", "tile"), check_vma=False)
```

```python
import functools

import jax
import jax.numpy as jnp
from jax import lax
from jax.experimental import pallas as pl
from jax.experimental.pallas import tpu as pltpu
from jax.sharding import PartitionSpec as P


FAC = 16
SWEEPS = 4
OMEGA = 0.8
MIX = 0.5
LANES = 128
SUB = 8
HALO = 8

VMEM = pl.BlockSpec(memory_space=pltpu.VMEM)


def limit(points):
    return 4 * 1024 * 1024 + 2048 * points


def call(points, body, shapes, count, scratch=()):
    return pl.pallas_call(
        body,
        out_shape=[jax.ShapeDtypeStruct(s, jnp.float32) for s in shapes],
        in_specs=[VMEM] * count,
        out_specs=[VMEM] * len(shapes),
        scratch_shapes=[pltpu.VMEM(s, jnp.float32) for s in scratch],
        compiler_params=pltpu.CompilerParams(vmem_limit_bytes=limit(points)),
    )


def lane_iota(shape):
    return lax.broadcasted_iota(jnp.int32, shape, len(shape) - 1)


def row_iota(shape):
    return lax.broadcasted_iota(jnp.int32, shape, 0)


def shift(x, by, axis):
    return pltpu.roll(x, by % x.shape[axis], axis)


def neighbour_sum(x):
    above, below = shift(x, 1, 0), shift(x, -1, 0)
    return above + below + shift(x + above, -1, 1) + shift(x + below, 1, 1)


def gather_lanes(x, index):
    return jnp.take_along_axis(x, index, axis=1)


def block_means(arrays):
    rows, cols = arrays[0].shape
    per_row = cols // FAC
    sums = [
        jnp.sum(x[a * FAC : (a + 1) * FAC], axis=0, keepdims=True)
        for x in arrays
        for a in range(rows // FAC)
    ]
    used = len(sums)
    high = jnp.concatenate(sums, axis=0)
    parts = []
    for _ in range(3):
        part = high.astype(jnp.bfloat16)
        parts.append(part.astype(jnp.float32))
        high = high - parts[-1]
    fill = -len(parts) * used % (2 * SUB)
    tall = jnp.concatenate(parts + [jnp.zeros((fill, cols), jnp.float32)], axis=0)
    pick = (
        lax.broadcasted_iota(jnp.int32, (cols, LANES), 0) // FAC
        == lax.rem(lane_iota((cols, LANES)), per_row)
    )
    line = jnp.dot(
        tall.astype(jnp.bfloat16),
        pick.astype(jnp.bfloat16),
        preferred_element_type=jnp.float32,
    )
    mine = lax.rem(row_iota(line.shape), used) == lax.rem(lane_iota(line.shape) // per_row, used)
    line = jnp.where(mine, line, 0.0)
    return jnp.sum(line, axis=0, keepdims=True) * (1.0 / (FAC * FAC))


def pack_lanes(strip, first):
    step = LANES // HALO
    parts = []
    for at in range(0, strip.shape[0], step):
        piece = strip[at : at + step]
        lane, row = lane_iota(piece.shape), row_iota(piece.shape)
        piece = gather_lanes(piece, first + lax.rem(lane, HALO))
        piece = jnp.where(lane // HALO == row, piece, 0.0)
        parts.append(jnp.sum(piece, axis=0, keepdims=True))
    return parts


def start_kernel(
    grid, rhs_in, diag_in, factor_in, slots_ref, rhs_ref, diag_ref, mine_ref, *rest
):
    edge_refs, sems = rest[:-1], rest[-1]
    here = factor_in.shape[0]
    factor_ref = mine_ref.at[:here, :]
    loads = [
        pltpu.make_async_copy(source, target, sems.at[k])
        for k, (source, target) in enumerate(
            ((rhs_in, rhs_ref), (diag_in, diag_ref), (factor_in, factor_ref))
        )
    ]
    for load in loads:
        load.start()
    groups, tiles = grid
    g, t = lax.axis_index("grp"), lax.axis_index("tile")
    rows, cols = rhs_ref.shape
    count = groups * tiles
    even = lax.rem(g, 2) == 0
    loads[0].wait()
    loads[1].wait()
    for at, ref in ((0, rhs_ref), (cols, diag_ref)):
        first, last = ref[:HALO, :], ref[rows - HALO :, :]
        mine_ref[here:, at : at + cols] = jnp.where(even, last, first)
        for edge_ref in edge_refs:
            edge_ref[:, at : at + cols] = jnp.where(even, first, last)
    coarse = block_means([rhs_ref[...], diag_ref[...]])
    to_left = lax.rem(row_iota((count, LANES)), tiles) < t
    lines = []
    for ref in (rhs_ref, diag_ref):
        left = pack_lanes(ref[:, :LANES], 0)
        right = pack_lanes(ref[:, cols - LANES :], LANES - HALO)
        lines += [jnp.where(to_left, one, two) for one, two in zip(left, right)]
    lines.append(jnp.broadcast_to(coarse, (count, LANES)))
    for k, line in enumerate(lines):
        slots_ref[pl.ds(k, count, stride=len(lines)), :] = line
    loads[2].wait()


def products(vector, factor_ref, here, first_lane=lambda m: m * LANES):
    total = None
    for m in range(vector.shape[0]):
        term = factor_ref[:here, pl.ds(first_lane(m), LANES)] * vector[m : m + 1, :]
        total = term if total is None else total + term
    return jnp.sum(total, axis=1, keepdims=True)


def interleave(even, odd):
    return jnp.where(lane_iota(even.shape) < LANES // 2, even, odd)


def pairs(ref, line, width):
    count = ref.shape[0] // width
    return [
        ref[pl.ds(line + side * width, count // 2, stride=2 * width), :] for side in range(2)
    ]


def inside_mask(grid, rows, cols):
    groups, tiles = grid
    g, t = lax.axis_index("grp"), lax.axis_index("tile")
    shape = (rows + 2 * HALO, cols + LANES)
    row, lane = row_iota(shape), lane_iota(shape)
    row_ok = (row < rows) | ((row < rows + HALO) & (g < groups - 1)) | ((row >= rows + HALO) & (g > 0))
    lane_ok = (
        (lane < cols)
        | ((lane < cols + HALO) & (t < tiles - 1))
        | ((lane >= cols + LANES - HALO) & (t > 0))
    )
    return row_ok & lane_ok


def unpack_lanes(got_ref, line, rows):
    step = LANES // HALO
    shape = (step, LANES)
    index = row_iota(shape) * HALO + lax.rem(lane_iota(shape), HALO)
    parts = []
    for k in range(rows // step):
        piece = jnp.broadcast_to(got_ref[pl.ds(line + k, 1), :], shape)
        parts.append(gather_lanes(piece, index))
    return jnp.concatenate(parts, axis=0)


def middle_kernel(
    grid, width, got_ref, rhs_ref, diag_ref, mine_ref, theirs_ref, *refs
):
    far_refs, outs = refs[:-8], refs[-8:]
    rhs_out, diag_out, weight_out, smooth_out, term_ref, ring_ref, slots_ref, term_scr = outs
    groups, tiles = grid
    g, t = lax.axis_index("grp"), lax.axis_index("tile")
    rows, cols = rhs_ref.shape
    here = mine_ref.shape[0] - HALO
    even, odd = pairs(got_ref, width - 1, width)
    mean = interleave(shift(even, LANES // 2, 1), odd)
    vector = interleave(even, shift(odd, LANES // 2, 1))
    inner = products(vector, mine_ref, here)
    other = products(vector, theirs_ref, here)
    for m in range(vector.shape[0]):
        place = slice(m * LANES, (m + 1) * LANES)
        term = mine_ref[:here, place] * inner + theirs_ref[:here, place] * other
        term_scr[m : m + 1, :] = jnp.sum(term, axis=0, keepdims=True)
    term = term_scr[...]
    coarse_grid = Coarse(term.shape, grid, (rows // FAC, cols // FAC))
    next_rhs = -MIX * coarse_operator(term, mean, coarse_grid)
    own = lax.rem(coarse_grid.group, 2) == lax.rem(g, 2)
    ends, columns = (jnp.where(own, x, 0.0) for x in around(term, coarse_grid))
    term = jnp.where(own, term, 0.0)
    half_lane = LANES // 2
    for k, x in enumerate((shift(term, half_lane, 1), term)):
        term_ref[k] = x
    ring_ref[0] = interleave(ends, shift(columns, half_lane, 1))
    ring_ref[1] = interleave(shift(ends, half_lane, 1), columns)
    near_ref = theirs_ref.at[here:, :]
    if groups > 2:
        near, far = near_ref[:, : 2 * cols], far_refs[0][...]
        is_even = lax.rem(g, 2) == 0
        below, above = jnp.where(is_even, near, far), jnp.where(is_even, far, near)
    else:
        below = above = near_ref[:, : 2 * cols]
    up, down = jnp.maximum(g - 1, 0), jnp.minimum(g + 1, groups - 1)
    left, right = jnp.maximum(t - 1, 0), jnp.minimum(t + 1, tiles - 1)
    inside = inside_mask(grid, rows, cols)
    at = 0
    for ref, out, edge in ((rhs_ref, rhs_out, 0), (diag_ref, diag_out, cols)):
        out[:rows, :cols] = ref[...]
        out[rows : rows + HALO, :cols] = below[:, edge : edge + cols]
        out[rows + HALO :, :cols] = above[:, edge : edge + cols]
        sides = []
        for column in (right, left):
            mid = unpack_lanes(got_ref, (g * tiles + column) * width + at, rows)
            low = unpack_lanes(got_ref, (down * tiles + column) * width + at, rows)[:HALO]
            top = unpack_lanes(got_ref, (up * tiles + column) * width + at, rows)[rows - HALO :]
            sides.append(jnp.concatenate([mid, low, top], axis=0))
        lane = lane_iota(sides[0].shape)
        side = jnp.where(lane < HALO, sides[0], 0.0)
        side = jnp.where(lane >= LANES - HALO, sides[1], side)
        out[:, cols:] = side
        at += rows * HALO // LANES
    rhs = jnp.where(inside, rhs_out[...], 0.0)
    diag = jnp.where(inside, diag_out[...], 0.0)
    rhs_out[...] = rhs
    diag_out[...] = diag
    weight = jnp.where(inside, OMEGA / (6.0 + diag), 0.0)
    weight_out[...] = weight
    smooth = weight * rhs
    for _ in range(SWEEPS - 1):
        smooth = (1.0 - OMEGA) * smooth + weight * (rhs + neighbour_sum(smooth))
    smooth_out[...] = smooth
    left_over = (rhs - (6.0 + diag) * smooth + neighbour_sum(smooth))[:rows, :cols]
    coarse = block_means([left_over])
    per_group = coarse_grid.per_group
    at = (g // 2) * tiles + t
    devices = LANES // here
    parity = lax.rem(g, 2)
    high = groups // 2 * per_group
    part = high // 2
    for k in range(2):
        half = jnp.concatenate(
            [
                next_rhs[m : m + per_group]
                for m in range(k * per_group, groups * per_group, 2 * per_group)
            ],
            axis=0,
        )
        place = row_iota(half.shape) * devices + lane_iota(half.shape) // here
        half = half + jnp.where((place == at) & (parity == k), coarse, 0.0)
        is_first = lax.rem(at * here // LANES // part + parity + k, 2) == 0
        sent = jnp.where(is_first, half[:part], half[part:])
        sent = jnp.concatenate([sent, sent], axis=0)
        for group in range(k, groups, 2):
            for device in range(group * tiles, (group + 1) * tiles, 2):
                slots_ref[device * part : (device + 2) * part, :] = sent


class Coarse:
    def __init__(self, shape, grid, blocks):
        self.groups, self.tiles = grid
        self.block_rows, self.per_row = blocks
        self.here = self.block_rows * self.per_row
        self.per_group = self.tiles * self.here // LANES
        self.lane = lane_iota(shape)
        device = row_iota(shape) * (LANES // self.here) + self.lane // self.here
        self.a = lax.rem(self.lane, self.here) // self.per_row
        self.b = lax.rem(self.lane, self.per_row)
        self.tile, self.group = lax.rem(device, self.tiles), device // self.tiles

    def left_of(self, x):
        near = shift(x, 1, 1)
        far = shift(x, self.here - self.per_row + 1, 1)
        far = jnp.where(self.lane < self.here, shift(far, 1, 0), far)
        return jnp.where(self.b > 0, near, jnp.where(self.tile > 0, far, 0.0))

    def right_of(self, x):
        near = shift(x, -1, 1)
        far = shift(x, -(self.here - self.per_row + 1), 1)
        far = jnp.where(self.lane >= LANES - self.here, shift(far, -1, 0), far)
        last = self.tile < self.tiles - 1
        return jnp.where(self.b < self.per_row - 1, near, jnp.where(last, far, 0.0))

    def above(self, x):
        near = shift(x, self.per_row, 1)
        far = shift(shift(x, -(self.here - self.per_row), 1), self.per_group, 0)
        return jnp.where(self.a > 0, near, jnp.where(self.group > 0, far, 0.0))

    def below(self, x):
        near = shift(x, -self.per_row, 1)
        far = shift(shift(x, self.here - self.per_row, 1), -self.per_group, 0)
        last = self.group < self.groups - 1
        return jnp.where(self.a < self.block_rows - 1, near, jnp.where(last, far, 0.0))


def coarse_operator(x, mean, coarse):
    above, below = coarse.above(x), coarse.below(x)
    sides = above + below + coarse.left_of(x) + coarse.right_of(x)
    corners = coarse.right_of(above) + coarse.left_of(below)
    edge = 2.0 * FAC - 1.0
    return mean * x + (edge * (4.0 * x - sides) + (2.0 * x - corners)) * (1.0 / (FAC * FAC))


def around(x, coarse):
    ends = jnp.where(coarse.a == 0, coarse.above(x), coarse.below(x))
    last = coarse.per_row - 1

    def sides(y):
        return jnp.where(coarse.b == 0, coarse.left_of(y), coarse.right_of(y))

    own, outer = sides(x), sides(ends)
    columns = jnp.where(coarse.b == 1, shift(outer, 1, 1), own)
    return ends, jnp.where(coarse.b == last - 1, shift(outer, -1, 1), columns)


def second_kernel(
    grid, per_group, got_ref, mine_ref, theirs_ref, term_ref, ring_ref, slots_ref, value_ref
):
    groups, tiles = grid
    parity = lax.rem(lax.axis_index("grp"), 2)
    here = mine_ref.shape[0] - HALO
    lines = mine_ref.shape[1] // LANES
    part = lines // 4
    sums = [None, None]
    for device in range(0, groups * tiles, 2):
        group, tile = device // tiles, device % tiles
        line = (group // 2 * tiles + tile) * here // LANES
        k = (line // part + group) % 2
        got = got_ref[device * part : (device + 2) * part, :]
        sums[k] = got if sums[k] is None else sums[k] + got
    one, two = [x[:part] + x[part:] for x in sums]
    coarse = jnp.concatenate(
        [jnp.where(parity == 0, one, two), jnp.where(parity == 0, two, one)], axis=0
    )

    def first_lane(m):
        line = (m // per_group * 2 + parity) * per_group + m % per_group
        return pl.multiple_of(line * LANES, LANES)

    inner = products(coarse, mine_ref, here, first_lane)
    other = products(coarse, theirs_ref, here, first_lane)
    for m in range(lines):
        place = slice(m * LANES, (m + 1) * LANES)
        term = mine_ref[:here, place] * inner + theirs_ref[:here, place] * other
        value_ref[m : m + 1, :] = jnp.sum(term, axis=0, keepdims=True)
    value = value_ref[...]
    slots_ref[pl.ds(0, lines, stride=4), :] = interleave(value, term_ref[0])
    slots_ref[pl.ds(1, lines, stride=4), :] = ring_ref[0]
    slots_ref[pl.ds(2, lines, stride=4), :] = interleave(shift(value, LANES // 2, 1), term_ref[1])
    slots_ref[pl.ds(3, lines, stride=4), :] = ring_ref[1]


def prolong_line(line, first, shape):
    index = jnp.broadcast_to(first + lane_iota(shape) // FAC, shape)
    return gather_lanes(jnp.broadcast_to(line, shape), index)


def last_kernel(grid, got_ref, rhs_ref, diag_ref, weight_ref, smooth_ref, out_ref, field_ref):
    rows, cols = out_ref.shape
    block_rows, per_row, per_tile = rows // FAC, cols // FAC, LANES // FAC
    here = block_rows * per_row
    inside = inside_mask(grid, rows, cols)
    shape = (SUB, LANES)
    total = got_ref[:SUB, :]
    for at in range(SUB, got_ref.shape[0], SUB):
        total = total + got_ref[at : at + SUB, :]
    total = total + shift(total, SUB // 2, 0)
    total = total + shift(total, SUB // 4, 0)
    second, ring = total[:1], total[1:2]

    def pick(line, at):
        return gather_lanes(jnp.broadcast_to(line, shape), jnp.full(shape, at, jnp.int32))

    bands = [(a * FAC, FAC, second, here + a * per_row, here + a * per_row) for a in range(block_rows)]
    bands += [(rows, HALO, ring, per_row, here + per_row), (rows + HALO, HALO, ring, 0, here)]
    for start, height, line, at, side in bands:
        parts = [prolong_line(line, at + q * per_tile, shape) for q in range(cols // LANES)]
        step = 0 if start < rows else 1
        beside, other = pick(ring, side + per_row - 1 - step), pick(ring, side + step)
        parts.append(jnp.where(lane_iota(shape) < LANES // 2, beside, other))
        for low in range(start, start + height, SUB):
            for q, part in enumerate(parts):
                field_ref[low : low + SUB, q * LANES : (q + 1) * LANES] = part
    field = jnp.where(inside, smooth_ref[...] + MIX * field_ref[...], 0.0)
    rhs = rhs_ref[...]
    weight = weight_ref[...]
    rest = rhs - (6.0 + diag_ref[...]) * field + neighbour_sum(field)
    smooth = weight * rest
    for _ in range(SWEEPS - 1):
        smooth = (1.0 - OMEGA) * smooth + weight * (rest + neighbour_sum(smooth))
    base = field[:rows, :cols] + smooth[:rows, :cols]
    line = MIX * second
    for a in range(rows // FAC):
        for q in range(cols // LANES):
            part = prolong_line(line, a * per_row + q * (LANES // FAC), (SUB, LANES))
            for low in range(a * FAC, (a + 1) * FAC, SUB):
                where = (slice(low, low + SUB), slice(q * LANES, (q + 1) * LANES))
                out_ref[where] = base[where] + part


def shards(right_side, diagonal, inverse_factor):
    groups, tiles = lax.axis_size("grp"), lax.axis_size("tile")
    grid = (groups, tiles)
    count = groups * tiles
    rows, cols = right_side.shape
    points = inverse_factor.shape[1]
    high = points // LANES
    assert 2 * inverse_factor.shape[0] == LANES and rows == 2 * FAC and groups % 2 == 0
    everyone = ("grp", "tile")

    def exchange(slots):
        lines = slots.shape[0] // count
        got = lax.all_to_all(slots.reshape(count, lines * LANES), everyone, 0, 0, tiled=True)
        return got.reshape(count * lines, LANES)

    width = 2 * rows * HALO // LANES + 1
    here = inverse_factor.shape[0]
    shapes = [(count * width, LANES), (rows, cols), (rows, cols), (here + HALO, points)]
    shapes += [(HALO, 2 * cols)] if groups > 2 else []
    slots, right_side, diagonal, mine, *edges = pl.pallas_call(
        functools.partial(start_kernel, grid),
        out_shape=[jax.ShapeDtypeStruct(s, jnp.float32) for s in shapes],
        in_specs=[pl.BlockSpec(memory_space=pltpu.HBM)] * 3,
        out_specs=[VMEM] * len(shapes),
        scratch_shapes=[pltpu.SemaphoreType.DMA((3,))],
        compiler_params=pltpu.CompilerParams(vmem_limit_bytes=limit(points)),
    )(
        *[
            pltpu.with_memory_space_constraint(x, pltpu.HBM)
            for x in (right_side, diagonal, inverse_factor)
        ]
    )
    theirs = lax.ppermute(mine, "grp", [(i, i ^ 1) for i in range(groups)])
    far = []
    if groups > 2:
        across = [(i, i + 1) for i in range(1, groups - 1, 2)]
        across += [(j, i) for i, j in across]
        far = [lax.ppermute(edges[0], "grp", across)]
    got = exchange(slots)

    wide = (rows + 2 * HALO, cols + LANES)
    rhs, diag, weight, smooth, term, ring, slots = call(
        points,
        functools.partial(middle_kernel, grid, width),
        [wide] * 4 + [(2, high, LANES)] * 2 + [(count * high // 4, LANES)],
        5 + len(far),
        [(high, LANES)],
    )(got, right_side, diagonal, mine, theirs, *far)
    got = exchange(slots)

    (slots,) = call(
        points,
        functools.partial(second_kernel, grid, high // groups),
        [(2 * count, LANES)],
        5,
        [(high, LANES)],
    )(got, mine, theirs, term, ring)
    got = exchange(slots)
    (field,) = call(
        points, functools.partial(last_kernel, grid), [(rows, cols)], 5, [wide]
    )(got, rhs, diag, weight, smooth)
    return field


def solution(mesh):
    placed = (P("grp", "tile"), P("grp", "tile"), P(("grp", "tile"), None))

    return jax.shard_map(
        shards, mesh=mesh, in_specs=placed, out_specs=P("grp", "tile"), check_vma=False
    )
```

```python
import functools

import jax
import jax.numpy as jnp
from jax import lax
from jax.experimental import pallas as pl
from jax.experimental.pallas import tpu as pltpu
from jax.sharding import PartitionSpec as P


FAC = 16
SWEEPS = 4
OMEGA = 0.8
MIX = 0.5
LANES = 128
SUB = 8
HALO = 8

VMEM = pl.BlockSpec(memory_space=pltpu.VMEM)


def limit(points):
    return 4 * 1024 * 1024 + 2048 * points


def call(points, body, shapes, count, scratch=()):
    return pl.pallas_call(
        body,
        out_shape=[jax.ShapeDtypeStruct(s, jnp.float32) for s in shapes],
        in_specs=[VMEM] * count,
        out_specs=[VMEM] * len(shapes),
        scratch_shapes=[pltpu.VMEM(s, jnp.float32) for s in scratch],
        compiler_params=pltpu.CompilerParams(vmem_limit_bytes=limit(points)),
    )


def lane_iota(shape):
    return lax.broadcasted_iota(jnp.int32, shape, len(shape) - 1)


def row_iota(shape):
    return lax.broadcasted_iota(jnp.int32, shape, 0)


def shift(x, by, axis):
    return pltpu.roll(x, by % x.shape[axis], axis)


def neighbour_sum(x):
    above, below = shift(x, 1, 0), shift(x, -1, 0)
    return above + below + shift(x + above, -1, 1) + shift(x + below, 1, 1)


def gather_lanes(x, index):
    return jnp.take_along_axis(x, index, axis=1)


def block_means(arrays):
    rows, cols = arrays[0].shape
    per_row = cols // FAC
    sums = [
        jnp.sum(x[a * FAC : (a + 1) * FAC], axis=0, keepdims=True)
        for x in arrays
        for a in range(rows // FAC)
    ]
    used = len(sums)
    high = jnp.concatenate(sums, axis=0)
    parts = []
    for _ in range(3):
        part = high.astype(jnp.bfloat16)
        parts.append(part.astype(jnp.float32))
        high = high - parts[-1]
    fill = -len(parts) * used % (2 * SUB)
    tall = jnp.concatenate(parts + [jnp.zeros((fill, cols), jnp.float32)], axis=0)
    pick = (
        lax.broadcasted_iota(jnp.int32, (cols, LANES), 0) // FAC
        == lax.rem(lane_iota((cols, LANES)), per_row)
    )
    line = jnp.dot(
        tall.astype(jnp.bfloat16),
        pick.astype(jnp.bfloat16),
        preferred_element_type=jnp.float32,
    )
    mine = lax.rem(row_iota(line.shape), used) == lax.rem(lane_iota(line.shape) // per_row, used)
    line = jnp.where(mine, line, 0.0)
    return jnp.sum(line, axis=0, keepdims=True) * (1.0 / (FAC * FAC))


def block_means_of(x):
    rows, cols = x.shape
    per_row = cols // FAC
    parts = []
    for _ in range(3):
        part = x.astype(jnp.bfloat16)
        parts.append(part)
        x = x - part.astype(jnp.float32)
    pick = (
        lax.broadcasted_iota(jnp.int32, (cols, LANES), 0) // FAC
        == lax.rem(lane_iota((cols, LANES)), per_row)
    )
    out = jnp.dot(
        jnp.concatenate(parts, axis=0),
        pick.astype(jnp.bfloat16),
        preferred_element_type=jnp.float32,
    )
    out = out[:rows] + out[rows : 2 * rows] + out[2 * rows :]
    used = rows // FAC
    mine = lax.rem(lane_iota((FAC, LANES)) // per_row, used)
    line = out[:FAC]
    for a in range(1, used):
        line = jnp.where(mine == a, out[a * FAC : (a + 1) * FAC], line)
    return jnp.sum(line, axis=0, keepdims=True) * (1.0 / (FAC * FAC))


def pack_lanes(strip, first):
    step = LANES // HALO
    parts = []
    for at in range(0, strip.shape[0], step):
        piece = strip[at : at + step]
        lane, row = lane_iota(piece.shape), row_iota(piece.shape)
        piece = gather_lanes(piece, first + lax.rem(lane, HALO))
        piece = jnp.where(lane // HALO == row, piece, 0.0)
        parts.append(jnp.sum(piece, axis=0, keepdims=True))
    return parts


def start_kernel(
    grid, rhs_in, diag_in, factor_in, slots_ref, rhs_ref, diag_ref, mine_ref, *rest
):
    edge_refs, sems = rest[:-1], rest[-1]
    here = factor_in.shape[0]
    factor_ref = mine_ref.at[:here, :]
    loads = [
        pltpu.make_async_copy(source, target, sems.at[k])
        for k, (source, target) in enumerate(
            ((rhs_in, rhs_ref), (diag_in, diag_ref), (factor_in, factor_ref))
        )
    ]
    for load in loads:
        load.start()
    groups, tiles = grid
    g, t = lax.axis_index("grp"), lax.axis_index("tile")
    rows, cols = rhs_ref.shape
    count = groups * tiles
    even = lax.rem(g, 2) == 0
    loads[0].wait()
    loads[1].wait()
    for at, ref in ((0, rhs_ref), (cols, diag_ref)):
        first, last = ref[:HALO, :], ref[rows - HALO :, :]
        mine_ref[here:, at : at + cols] = jnp.where(even, last, first)
        for edge_ref in edge_refs:
            edge_ref[:, at : at + cols] = jnp.where(even, first, last)
    coarse = block_means([rhs_ref[...], diag_ref[...]])
    to_left = lax.rem(row_iota((count, LANES)), tiles) < t
    lines = []
    for ref in (rhs_ref, diag_ref):
        left = pack_lanes(ref[:, :LANES], 0)
        right = pack_lanes(ref[:, cols - LANES :], LANES - HALO)
        lines += [jnp.where(to_left, one, two) for one, two in zip(left, right)]
    lines.append(jnp.broadcast_to(coarse, (count, LANES)))
    for k, line in enumerate(lines):
        slots_ref[pl.ds(k, count, stride=len(lines)), :] = line
    loads[2].wait()


def products(vector, factor_ref, here, first_lane=lambda m: m * LANES):
    total = None
    for m in range(vector.shape[0]):
        term = factor_ref[:here, pl.ds(first_lane(m), LANES)] * vector[m : m + 1, :]
        total = term if total is None else total + term
    return jnp.sum(total, axis=1, keepdims=True)


def interleave(even, odd):
    return jnp.where(lane_iota(even.shape) < LANES // 2, even, odd)


def pairs(ref, line, width):
    count = ref.shape[0] // width
    return [
        ref[pl.ds(line + side * width, count // 2, stride=2 * width), :] for side in range(2)
    ]


def inside_mask(grid, rows, cols):
    groups, tiles = grid
    g, t = lax.axis_index("grp"), lax.axis_index("tile")
    shape = (rows + 2 * HALO, cols + LANES)
    row, lane = row_iota(shape), lane_iota(shape)
    row_ok = (row < rows) | ((row < rows + HALO) & (g < groups - 1)) | ((row >= rows + HALO) & (g > 0))
    lane_ok = (
        (lane < cols)
        | ((lane < cols + HALO) & (t < tiles - 1))
        | ((lane >= cols + LANES - HALO) & (t > 0))
    )
    return row_ok & lane_ok


def unpack_lanes(got_ref, line, rows):
    step = LANES // HALO
    shape = (step, LANES)
    index = row_iota(shape) * HALO + lax.rem(lane_iota(shape), HALO)
    parts = []
    for k in range(rows // step):
        piece = jnp.broadcast_to(got_ref[pl.ds(line + k, 1), :], shape)
        parts.append(gather_lanes(piece, index))
    return jnp.concatenate(parts, axis=0)


def middle_kernel(
    grid, width, got_ref, rhs_ref, diag_ref, mine_ref, theirs_ref, *refs
):
    far_refs, outs = refs[:-8], refs[-8:]
    rhs_out, diag_out, weight_out, smooth_out, term_ref, ring_ref, slots_ref, term_scr = outs
    groups, tiles = grid
    g, t = lax.axis_index("grp"), lax.axis_index("tile")
    rows, cols = rhs_ref.shape
    here = mine_ref.shape[0] - HALO
    even, odd = pairs(got_ref, width - 1, width)
    mean = interleave(shift(even, LANES // 2, 1), odd)
    vector = interleave(even, shift(odd, LANES // 2, 1))
    inner = products(vector, mine_ref, here)
    other = products(vector, theirs_ref, here)
    for m in range(vector.shape[0]):
        place = slice(m * LANES, (m + 1) * LANES)
        term = mine_ref[:here, place] * inner + theirs_ref[:here, place] * other
        term_scr[m : m + 1, :] = jnp.sum(term, axis=0, keepdims=True)
    term = term_scr[...]
    coarse_grid = Coarse(term.shape, grid, (rows // FAC, cols // FAC))
    next_rhs = -MIX * coarse_operator(term, mean, coarse_grid)
    own = lax.rem(coarse_grid.group, 2) == lax.rem(g, 2)
    ends, columns = (jnp.where(own, x, 0.0) for x in around(term, coarse_grid))
    term = jnp.where(own, term, 0.0)
    half_lane = LANES // 2
    for k, x in enumerate((shift(term, half_lane, 1), term)):
        term_ref[k] = x
    ring_ref[0] = interleave(ends, shift(columns, half_lane, 1))
    ring_ref[1] = interleave(shift(ends, half_lane, 1), columns)
    near_ref = theirs_ref.at[here:, :]
    if groups > 2:
        near, far = near_ref[:, : 2 * cols], far_refs[0][...]
        is_even = lax.rem(g, 2) == 0
        below, above = jnp.where(is_even, near, far), jnp.where(is_even, far, near)
    else:
        below = above = near_ref[:, : 2 * cols]
    up, down = jnp.maximum(g - 1, 0), jnp.minimum(g + 1, groups - 1)
    left, right = jnp.maximum(t - 1, 0), jnp.minimum(t + 1, tiles - 1)
    inside = inside_mask(grid, rows, cols)
    at = 0
    for ref, out, edge in ((rhs_ref, rhs_out, 0), (diag_ref, diag_out, cols)):
        out[:rows, :cols] = ref[...]
        out[rows : rows + HALO, :cols] = below[:, edge : edge + cols]
        out[rows + HALO :, :cols] = above[:, edge : edge + cols]
        sides = []
        for column in (right, left):
            mid = unpack_lanes(got_ref, (g * tiles + column) * width + at, rows)
            low = unpack_lanes(got_ref, (down * tiles + column) * width + at, rows)[:HALO]
            top = unpack_lanes(got_ref, (up * tiles + column) * width + at, rows)[rows - HALO :]
            sides.append(jnp.concatenate([mid, low, top], axis=0))
        lane = lane_iota(sides[0].shape)
        side = jnp.where(lane < HALO, sides[0], 0.0)
        side = jnp.where(lane >= LANES - HALO, sides[1], side)
        out[:, cols:] = side
        at += rows * HALO // LANES
    rhs = jnp.where(inside, rhs_out[...], 0.0)
    diag = jnp.where(inside, diag_out[...], 0.0)
    rhs_out[...] = rhs
    diag_out[...] = diag
    weight = jnp.where(inside, OMEGA / (6.0 + diag), 0.0)
    weight_out[...] = weight
    smooth = weight * rhs
    for _ in range(SWEEPS - 1):
        smooth = (1.0 - OMEGA) * smooth + weight * (rhs + neighbour_sum(smooth))
    smooth_out[...] = smooth
    left_over = (rhs - (6.0 + diag) * smooth + neighbour_sum(smooth))[:rows, :cols]
    coarse = block_means_of(left_over)
    per_group = coarse_grid.per_group
    at = (g // 2) * tiles + t
    devices = LANES // here
    parity = lax.rem(g, 2)
    high = groups // 2 * per_group
    part = high // 2
    for k in range(2):
        half = jnp.concatenate(
            [
                next_rhs[m : m + per_group]
                for m in range(k * per_group, groups * per_group, 2 * per_group)
            ],
            axis=0,
        )
        place = row_iota(half.shape) * devices + lane_iota(half.shape) // here
        half = half + jnp.where((place == at) & (parity == k), coarse, 0.0)
        is_first = lax.rem(at * here // LANES // part + parity + k, 2) == 0
        sent = jnp.where(is_first, half[:part], half[part:])
        sent = jnp.concatenate([sent, sent], axis=0)
        for group in range(k, groups, 2):
            for device in range(group * tiles, (group + 1) * tiles, 2):
                slots_ref[device * part : (device + 2) * part, :] = sent


class Coarse:
    def __init__(self, shape, grid, blocks):
        self.groups, self.tiles = grid
        self.block_rows, self.per_row = blocks
        self.here = self.block_rows * self.per_row
        self.per_group = self.tiles * self.here // LANES
        self.lane = lane_iota(shape)
        device = row_iota(shape) * (LANES // self.here) + self.lane // self.here
        self.a = lax.rem(self.lane, self.here) // self.per_row
        self.b = lax.rem(self.lane, self.per_row)
        self.tile, self.group = lax.rem(device, self.tiles), device // self.tiles

    def left_of(self, x):
        near = shift(x, 1, 1)
        far = shift(x, self.here - self.per_row + 1, 1)
        far = jnp.where(self.lane < self.here, shift(far, 1, 0), far)
        return jnp.where(self.b > 0, near, jnp.where(self.tile > 0, far, 0.0))

    def right_of(self, x):
        near = shift(x, -1, 1)
        far = shift(x, -(self.here - self.per_row + 1), 1)
        far = jnp.where(self.lane >= LANES - self.here, shift(far, -1, 0), far)
        last = self.tile < self.tiles - 1
        return jnp.where(self.b < self.per_row - 1, near, jnp.where(last, far, 0.0))

    def above(self, x):
        near = shift(x, self.per_row, 1)
        far = shift(shift(x, -(self.here - self.per_row), 1), self.per_group, 0)
        return jnp.where(self.a > 0, near, jnp.where(self.group > 0, far, 0.0))

    def below(self, x):
        near = shift(x, -self.per_row, 1)
        far = shift(shift(x, self.here - self.per_row, 1), -self.per_group, 0)
        last = self.group < self.groups - 1
        return jnp.where(self.a < self.block_rows - 1, near, jnp.where(last, far, 0.0))


def coarse_operator(x, mean, coarse):
    above, below = coarse.above(x), coarse.below(x)
    sides = above + below + coarse.left_of(x) + coarse.right_of(x)
    corners = coarse.right_of(above) + coarse.left_of(below)
    edge = 2.0 * FAC - 1.0
    return mean * x + (edge * (4.0 * x - sides) + (2.0 * x - corners)) * (1.0 / (FAC * FAC))


def around(x, coarse):
    ends = jnp.where(coarse.a == 0, coarse.above(x), coarse.below(x))
    last = coarse.per_row - 1

    def sides(y):
        return jnp.where(coarse.b == 0, coarse.left_of(y), coarse.right_of(y))

    own, outer = sides(x), sides(ends)
    columns = jnp.where(coarse.b == 1, shift(outer, 1, 1), own)
    return ends, jnp.where(coarse.b == last - 1, shift(outer, -1, 1), columns)


def second_kernel(
    grid, per_group, got_ref, mine_ref, theirs_ref, term_ref, ring_ref, slots_ref, value_ref
):
    groups, tiles = grid
    parity = lax.rem(lax.axis_index("grp"), 2)
    here = mine_ref.shape[0] - HALO
    lines = mine_ref.shape[1] // LANES
    part = lines // 4
    sums = [None, None]
    for device in range(0, groups * tiles, 2):
        group, tile = device // tiles, device % tiles
        line = (group // 2 * tiles + tile) * here // LANES
        k = (line // part + group) % 2
        got = got_ref[device * part : (device + 2) * part, :]
        sums[k] = got if sums[k] is None else sums[k] + got
    one, two = [x[:part] + x[part:] for x in sums]
    coarse = jnp.concatenate(
        [jnp.where(parity == 0, one, two), jnp.where(parity == 0, two, one)], axis=0
    )

    def first_lane(m):
        line = (m // per_group * 2 + parity) * per_group + m % per_group
        return pl.multiple_of(line * LANES, LANES)

    inner = products(coarse, mine_ref, here, first_lane)
    other = products(coarse, theirs_ref, here, first_lane)
    for m in range(lines):
        place = slice(m * LANES, (m + 1) * LANES)
        term = mine_ref[:here, place] * inner + theirs_ref[:here, place] * other
        value_ref[m : m + 1, :] = jnp.sum(term, axis=0, keepdims=True)
    value = value_ref[...]
    slots_ref[pl.ds(0, lines, stride=4), :] = interleave(value, term_ref[0])
    slots_ref[pl.ds(1, lines, stride=4), :] = ring_ref[0]
    slots_ref[pl.ds(2, lines, stride=4), :] = interleave(shift(value, LANES // 2, 1), term_ref[1])
    slots_ref[pl.ds(3, lines, stride=4), :] = ring_ref[1]


def prolong_line(line, first, shape):
    index = jnp.broadcast_to(first + lane_iota(shape) // FAC, shape)
    return gather_lanes(jnp.broadcast_to(line, shape), index)


def last_kernel(grid, got_ref, rhs_ref, diag_ref, weight_ref, smooth_ref, out_ref):
    rows, cols = out_ref.shape
    block_rows, per_row, per_tile = rows // FAC, cols // FAC, LANES // FAC
    here = block_rows * per_row
    shape = (SUB, LANES)
    lane = lane_iota(shape)
    g, t = lax.axis_index("grp"), lax.axis_index("tile")
    in_side = ((lane < HALO) & (t < grid[1] - 1)) | ((lane >= LANES - HALO) & (t > 0))
    total = got_ref[:SUB, :]
    for at in range(SUB, got_ref.shape[0], SUB):
        total = total + got_ref[at : at + SUB, :]
    total = total + shift(total, SUB // 2, 0)
    total = total + shift(total, SUB // 4, 0)
    second, ring = total[:1], total[1:2]

    def pick(line, at):
        return gather_lanes(jnp.broadcast_to(line, shape), jnp.full(shape, at, jnp.int32))

    def band(line, at, side, step):
        parts = [prolong_line(line, at + q * per_tile, shape) for q in range(cols // LANES)]
        beside, other = pick(ring, side + per_row - 1 - step), pick(ring, side + step)
        return parts + [jnp.where(in_side, jnp.where(lane < LANES // 2, beside, other), 0.0)]

    bands = [band(second, here + a * per_row, here + a * per_row, 0) for a in range(block_rows)]
    under = [jnp.where(g < grid[0] - 1, x, 0.0) for x in band(ring, per_row, here + per_row, 1)]
    over = [jnp.where(g > 0, x, 0.0) for x in band(ring, 0, here, 1)]
    tiles = [bands[at // FAC] for at in range(0, rows, SUB)] + [under, over]
    field = jnp.concatenate(
        [jnp.concatenate([tile[q] for tile in tiles], axis=0) for q in range(len(over))], axis=1
    )
    field = smooth_ref[...] + MIX * field
    rhs = rhs_ref[...]
    weight = weight_ref[...]
    rest = rhs - (6.0 + diag_ref[...]) * field + neighbour_sum(field)
    smooth = weight * rest
    for _ in range(SWEEPS - 1):
        smooth = (1.0 - OMEGA) * smooth + weight * (rest + neighbour_sum(smooth))
    base = field[:rows, :cols] + smooth[:rows, :cols]
    line = MIX * second
    for a in range(rows // FAC):
        for q in range(cols // LANES):
            part = prolong_line(line, a * per_row + q * (LANES // FAC), (SUB, LANES))
            for low in range(a * FAC, (a + 1) * FAC, SUB):
                where = (slice(low, low + SUB), slice(q * LANES, (q + 1) * LANES))
                out_ref[where] = base[where] + part


def shards(right_side, diagonal, inverse_factor):
    groups, tiles = lax.axis_size("grp"), lax.axis_size("tile")
    grid = (groups, tiles)
    count = groups * tiles
    rows, cols = right_side.shape
    points = inverse_factor.shape[1]
    high = points // LANES
    assert 2 * inverse_factor.shape[0] == LANES and rows == 2 * FAC and groups % 2 == 0
    everyone = ("grp", "tile")

    def exchange(slots):
        lines = slots.shape[0] // count
        got = lax.all_to_all(slots.reshape(count, lines * LANES), everyone, 0, 0, tiled=True)
        return got.reshape(count * lines, LANES)

    width = 2 * rows * HALO // LANES + 1
    here = inverse_factor.shape[0]
    shapes = [(count * width, LANES), (rows, cols), (rows, cols), (here + HALO, points)]
    shapes += [(HALO, 2 * cols)] if groups > 2 else []
    slots, right_side, diagonal, mine, *edges = pl.pallas_call(
        functools.partial(start_kernel, grid),
        out_shape=[jax.ShapeDtypeStruct(s, jnp.float32) for s in shapes],
        in_specs=[pl.BlockSpec(memory_space=pltpu.HBM)] * 3,
        out_specs=[VMEM] * len(shapes),
        scratch_shapes=[pltpu.SemaphoreType.DMA((3,))],
        compiler_params=pltpu.CompilerParams(vmem_limit_bytes=limit(points)),
    )(
        *[
            pltpu.with_memory_space_constraint(x, pltpu.HBM)
            for x in (right_side, diagonal, inverse_factor)
        ]
    )
    theirs = lax.ppermute(mine, "grp", [(i, i ^ 1) for i in range(groups)])
    far = []
    if groups > 2:
        across = [(i, i + 1) for i in range(1, groups - 1, 2)]
        across += [(j, i) for i, j in across]
        far = [lax.ppermute(edges[0], "grp", across)]
    got = exchange(slots)

    wide = (rows + 2 * HALO, cols + LANES)
    rhs, diag, weight, smooth, term, ring, slots = call(
        points,
        functools.partial(middle_kernel, grid, width),
        [wide] * 4 + [(2, high, LANES)] * 2 + [(count * high // 4, LANES)],
        5 + len(far),
        [(high, LANES)],
    )(got, right_side, diagonal, mine, theirs, *far)
    got = exchange(slots)

    (slots,) = call(
        points,
        functools.partial(second_kernel, grid, high // groups),
        [(2 * count, LANES)],
        5,
        [(high, LANES)],
    )(got, mine, theirs, term, ring)
    got = exchange(slots)
    (field,) = call(
        points, functools.partial(last_kernel, grid), [(rows, cols)], 5
    )(got, rhs, diag, weight, smooth)
    return field


def solution(mesh):
    placed = (P("grp", "tile"), P("grp", "tile"), P(("grp", "tile"), None))

    return jax.shard_map(
        shards, mesh=mesh, in_specs=placed, out_specs=P("grp", "tile"), check_vma=False
    )
```

```python
import functools

import jax
import jax.numpy as jnp
from jax import lax
from jax.experimental import pallas as pl
from jax.experimental.pallas import tpu as pltpu
from jax.sharding import PartitionSpec as P


FAC = 16
SWEEPS = 4
OMEGA = 0.8
MIX = 0.5
LANES = 128
SUB = 8
HALO = 8

VMEM = pl.BlockSpec(memory_space=pltpu.VMEM)


def limit(points):
    return 4 * 1024 * 1024 + 2048 * points


def call(points, body, shapes, count, scratch=()):
    return pl.pallas_call(
        body,
        out_shape=[jax.ShapeDtypeStruct(s, jnp.float32) for s in shapes],
        in_specs=[VMEM] * count,
        out_specs=[VMEM] * len(shapes),
        scratch_shapes=[pltpu.VMEM(s, jnp.float32) for s in scratch],
        compiler_params=pltpu.CompilerParams(vmem_limit_bytes=limit(points)),
    )


def lane_iota(shape):
    return lax.broadcasted_iota(jnp.int32, shape, len(shape) - 1)


def row_iota(shape):
    return lax.broadcasted_iota(jnp.int32, shape, 0)


def shift(x, by, axis):
    return pltpu.roll(x, by % x.shape[axis], axis)


def neighbour_sum(x):
    above, below = shift(x, 1, 0), shift(x, -1, 0)
    return above + below + shift(x + above, -1, 1) + shift(x + below, 1, 1)


def gather_lanes(x, index):
    return jnp.take_along_axis(x, index, axis=1)


def block_means(arrays):
    rows, cols = arrays[0].shape
    per_row = cols // FAC
    sums = [
        jnp.sum(x[a * FAC : (a + 1) * FAC], axis=0, keepdims=True)
        for x in arrays
        for a in range(rows // FAC)
    ]
    used = len(sums)
    high = jnp.concatenate(sums, axis=0)
    parts = []
    for _ in range(3):
        part = high.astype(jnp.bfloat16)
        parts.append(part.astype(jnp.float32))
        high = high - parts[-1]
    fill = -len(parts) * used % (2 * SUB)
    tall = jnp.concatenate(parts + [jnp.zeros((fill, cols), jnp.float32)], axis=0)
    pick = (
        lax.broadcasted_iota(jnp.int32, (cols, LANES), 0) // FAC
        == lax.rem(lane_iota((cols, LANES)), per_row)
    )
    line = jnp.dot(
        tall.astype(jnp.bfloat16),
        pick.astype(jnp.bfloat16),
        preferred_element_type=jnp.float32,
    )
    mine = lax.rem(row_iota(line.shape), used) == lax.rem(lane_iota(line.shape) // per_row, used)
    line = jnp.where(mine, line, 0.0)
    return jnp.sum(line, axis=0, keepdims=True) * (1.0 / (FAC * FAC))


def block_means_of(x):
    rows, cols = x.shape
    per_row = cols // FAC
    parts = []
    for _ in range(3):
        part = x.astype(jnp.bfloat16)
        parts.append(part)
        x = x - part.astype(jnp.float32)
    pick = (
        lax.broadcasted_iota(jnp.int32, (cols, LANES), 0) // FAC
        == lax.rem(lane_iota((cols, LANES)), per_row)
    )
    out = jnp.dot(
        jnp.concatenate(parts, axis=0),
        pick.astype(jnp.bfloat16),
        preferred_element_type=jnp.float32,
    )
    out = out[:rows] + out[rows : 2 * rows] + out[2 * rows :]
    used = rows // FAC
    mine = lax.rem(lane_iota((FAC, LANES)) // per_row, used)
    line = out[:FAC]
    for a in range(1, used):
        line = jnp.where(mine == a, out[a * FAC : (a + 1) * FAC], line)
    return jnp.sum(line, axis=0, keepdims=True) * (1.0 / (FAC * FAC))


def pack_lanes(strip, first):
    step = LANES // HALO
    parts = []
    for at in range(0, strip.shape[0], step):
        piece = strip[at : at + step]
        lane, row = lane_iota(piece.shape), row_iota(piece.shape)
        piece = gather_lanes(piece, first + lax.rem(lane, HALO))
        piece = jnp.where(lane // HALO == row, piece, 0.0)
        parts.append(jnp.sum(piece, axis=0, keepdims=True))
    return parts


def start_kernel(
    grid, rhs_in, diag_in, factor_in, slots_ref, rhs_ref, diag_ref, mine_ref, *rest
):
    edge_refs, sems = rest[:-1], rest[-1]
    here = factor_in.shape[0]
    factor_ref = mine_ref.at[:here, :]
    loads = [
        pltpu.make_async_copy(source, target, sems.at[k])
        for k, (source, target) in enumerate(
            ((rhs_in, rhs_ref), (diag_in, diag_ref), (factor_in, factor_ref))
        )
    ]
    for load, priority in zip(loads, (0, 0, 1)):
        load.start(priority=priority)
    groups, tiles = grid
    g, t = lax.axis_index("grp"), lax.axis_index("tile")
    rows, cols = rhs_ref.shape
    count = groups * tiles
    even = lax.rem(g, 2) == 0
    loads[0].wait()
    loads[1].wait()
    for at, ref in ((0, rhs_ref), (cols, diag_ref)):
        first, last = ref[:HALO, :], ref[rows - HALO :, :]
        mine_ref[here:, at : at + cols] = jnp.where(even, last, first)
        for edge_ref in edge_refs:
            edge_ref[:, at : at + cols] = jnp.where(even, first, last)
    coarse = block_means([rhs_ref[...], diag_ref[...]])
    to_left = lax.rem(row_iota((count, LANES)), tiles) < t
    lines = []
    for ref in (rhs_ref, diag_ref):
        left = pack_lanes(ref[:, :LANES], 0)
        right = pack_lanes(ref[:, cols - LANES :], LANES - HALO)
        lines += [jnp.where(to_left, one, two) for one, two in zip(left, right)]
    lines.append(jnp.broadcast_to(coarse, (count, LANES)))
    for k, line in enumerate(lines):
        slots_ref[pl.ds(k, count, stride=len(lines)), :] = line
    loads[2].wait()


def products(vector, factor_ref, here, first_lane=lambda m: m * LANES):
    total = None
    for m in range(vector.shape[0]):
        term = factor_ref[:here, pl.ds(first_lane(m), LANES)] * vector[m : m + 1, :]
        total = term if total is None else total + term
    return jnp.sum(total, axis=1, keepdims=True)


def interleave(even, odd):
    return jnp.where(lane_iota(even.shape) < LANES // 2, even, odd)


def pairs(ref, line, width):
    count = ref.shape[0] // width
    return [
        ref[pl.ds(line + side * width, count // 2, stride=2 * width), :] for side in range(2)
    ]


def lane_inside(grid, lane):
    t = lax.axis_index("tile")
    return ((lane < HALO) & (t < grid[1] - 1)) | ((lane >= LANES - HALO) & (t > 0))


def unpack_lanes(got_ref, line, rows):
    step = LANES // HALO
    shape = (step, LANES)
    index = row_iota(shape) * HALO + lax.rem(lane_iota(shape), HALO)
    parts = []
    for k in range(rows // step):
        piece = jnp.broadcast_to(got_ref[pl.ds(line + k, 1), :], shape)
        parts.append(gather_lanes(piece, index))
    return jnp.concatenate(parts, axis=0)


def middle_kernel(
    grid, width, got_ref, rhs_ref, diag_ref, mine_ref, theirs_ref, *refs
):
    far_refs, outs = refs[:-8], refs[-8:]
    rhs_out, diag_out, weight_out, smooth_out, term_ref, ring_ref, slots_ref, term_scr = outs
    groups, tiles = grid
    g, t = lax.axis_index("grp"), lax.axis_index("tile")
    rows, cols = rhs_ref.shape
    here = mine_ref.shape[0] - HALO
    even, odd = pairs(got_ref, width - 1, width)
    mean = interleave(shift(even, LANES // 2, 1), odd)
    vector = interleave(even, shift(odd, LANES // 2, 1))
    inner = products(vector, mine_ref, here)
    other = products(vector, theirs_ref, here)
    for m in range(vector.shape[0]):
        place = slice(m * LANES, (m + 1) * LANES)
        term = mine_ref[:here, place] * inner + theirs_ref[:here, place] * other
        term_scr[m : m + 1, :] = jnp.sum(term, axis=0, keepdims=True)
    term = term_scr[...]
    coarse_grid = Coarse(term.shape, grid, (rows // FAC, cols // FAC))
    next_rhs = -MIX * coarse_operator(term, mean, coarse_grid)
    own = lax.rem(coarse_grid.group, 2) == lax.rem(g, 2)
    ends, columns = (jnp.where(own, x, 0.0) for x in around(term, coarse_grid))
    term = jnp.where(own, term, 0.0)
    half_lane = LANES // 2
    for k, x in enumerate((shift(term, half_lane, 1), term)):
        term_ref[k] = x
    ring_ref[0] = interleave(ends, shift(columns, half_lane, 1))
    ring_ref[1] = interleave(shift(ends, half_lane, 1), columns)
    near_ref = theirs_ref.at[here:, :]
    if groups > 2:
        near, far = near_ref[:, : 2 * cols], far_refs[0][...]
        is_even = lax.rem(g, 2) == 0
        below, above = jnp.where(is_even, near, far), jnp.where(is_even, far, near)
    else:
        below = above = near_ref[:, : 2 * cols]
    up, down = jnp.maximum(g - 1, 0), jnp.minimum(g + 1, groups - 1)
    left, right = jnp.maximum(t - 1, 0), jnp.minimum(t + 1, tiles - 1)
    shape = (rows + 2 * HALO, LANES)
    lane, row = lane_iota(shape), row_iota(shape)
    is_right = lane < LANES // 2
    in_rows = (row < rows) | ((row < rows + HALO) & (g < groups - 1)) | ((row >= rows + HALO) & (g > 0))
    in_side = in_rows & lane_inside(grid, lane)

    def frame(own, under, over, side):
        return jnp.concatenate([jnp.concatenate([own, under, over], axis=0), side], axis=1)

    at = 0
    parts = []
    for ref, edge in ((rhs_ref, 0), (diag_ref, cols)):
        sides = []
        for column in (right, left):
            mid = unpack_lanes(got_ref, (g * tiles + column) * width + at, rows)
            low = unpack_lanes(got_ref, (down * tiles + column) * width + at, rows)[:HALO]
            top = unpack_lanes(got_ref, (up * tiles + column) * width + at, rows)[rows - HALO :]
            sides.append(jnp.concatenate([mid, low, top], axis=0))
        parts.append(
            (
                ref[...],
                jnp.where(g < groups - 1, below[:, edge : edge + cols], 0.0),
                jnp.where(g > 0, above[:, edge : edge + cols], 0.0),
                jnp.where(in_side, jnp.where(is_right, *sides), 0.0),
            )
        )
        at += rows * HALO // LANES
    rhs, diag = frame(*parts[0]), frame(*parts[1])
    own_w, under_w, over_w, side_w = [OMEGA / (6.0 + x) for x in parts[1]]
    weight = frame(
        own_w,
        jnp.where(g < groups - 1, under_w, 0.0),
        jnp.where(g > 0, over_w, 0.0),
        jnp.where(in_side, side_w, 0.0),
    )
    smooth = weight * rhs
    for _ in range(SWEEPS - 1):
        smooth = (1.0 - OMEGA) * smooth + weight * (rhs + neighbour_sum(smooth))
    for x, out in ((rhs, rhs_out), (diag, diag_out), (weight, weight_out), (smooth, smooth_out)):
        out[...] = x
    left_over = (rhs - (6.0 + diag) * smooth + neighbour_sum(smooth))[:rows, :cols]
    coarse = block_means_of(left_over)
    per_group = coarse_grid.per_group
    at = (g // 2) * tiles + t
    devices = LANES // here
    parity = lax.rem(g, 2)
    high = groups // 2 * per_group
    part = high // 2
    for k in range(2):
        half = jnp.concatenate(
            [
                next_rhs[m : m + per_group]
                for m in range(k * per_group, groups * per_group, 2 * per_group)
            ],
            axis=0,
        )
        place = row_iota(half.shape) * devices + lane_iota(half.shape) // here
        half = half + jnp.where((place == at) & (parity == k), coarse, 0.0)
        is_first = lax.rem(at * here // LANES // part + parity + k, 2) == 0
        sent = jnp.where(is_first, half[:part], half[part:])
        sent = jnp.concatenate([sent, sent], axis=0)
        for group in range(k, groups, 2):
            for device in range(group * tiles, (group + 1) * tiles, 2):
                slots_ref[device * part : (device + 2) * part, :] = sent


class Coarse:
    def __init__(self, shape, grid, blocks):
        self.groups, self.tiles = grid
        self.block_rows, self.per_row = blocks
        self.here = self.block_rows * self.per_row
        self.per_group = self.tiles * self.here // LANES
        self.lane = lane_iota(shape)
        device = row_iota(shape) * (LANES // self.here) + self.lane // self.here
        self.a = lax.rem(self.lane, self.here) // self.per_row
        self.b = lax.rem(self.lane, self.per_row)
        self.tile, self.group = lax.rem(device, self.tiles), device // self.tiles

    def left_of(self, x):
        near = shift(x, 1, 1)
        far = shift(x, self.here - self.per_row + 1, 1)
        far = jnp.where(self.lane < self.here, shift(far, 1, 0), far)
        return jnp.where(self.b > 0, near, jnp.where(self.tile > 0, far, 0.0))

    def right_of(self, x):
        near = shift(x, -1, 1)
        far = shift(x, -(self.here - self.per_row + 1), 1)
        far = jnp.where(self.lane >= LANES - self.here, shift(far, -1, 0), far)
        last = self.tile < self.tiles - 1
        return jnp.where(self.b < self.per_row - 1, near, jnp.where(last, far, 0.0))

    def above(self, x):
        near = shift(x, self.per_row, 1)
        far = shift(shift(x, -(self.here - self.per_row), 1), self.per_group, 0)
        return jnp.where(self.a > 0, near, jnp.where(self.group > 0, far, 0.0))

    def below(self, x):
        near = shift(x, -self.per_row, 1)
        far = shift(shift(x, self.here - self.per_row, 1), -self.per_group, 0)
        last = self.group < self.groups - 1
        return jnp.where(self.a < self.block_rows - 1, near, jnp.where(last, far, 0.0))


def coarse_operator(x, mean, coarse):
    above, below = coarse.above(x), coarse.below(x)
    sides = above + below + coarse.left_of(x) + coarse.right_of(x)
    corners = coarse.right_of(above) + coarse.left_of(below)
    edge = 2.0 * FAC - 1.0
    return mean * x + (edge * (4.0 * x - sides) + (2.0 * x - corners)) * (1.0 / (FAC * FAC))


def around(x, coarse):
    ends = jnp.where(coarse.a == 0, coarse.above(x), coarse.below(x))
    last = coarse.per_row - 1

    def sides(y):
        return jnp.where(coarse.b == 0, coarse.left_of(y), coarse.right_of(y))

    own, outer = sides(x), sides(ends)
    columns = jnp.where(coarse.b == 1, shift(outer, 1, 1), own)
    return ends, jnp.where(coarse.b == last - 1, shift(outer, -1, 1), columns)


def second_kernel(
    grid, per_group, got_ref, mine_ref, theirs_ref, term_ref, ring_ref, slots_ref, value_ref
):
    groups, tiles = grid
    parity = lax.rem(lax.axis_index("grp"), 2)
    here = mine_ref.shape[0] - HALO
    lines = mine_ref.shape[1] // LANES
    part = lines // 4
    sums = [None, None]
    for device in range(0, groups * tiles, 2):
        group, tile = device // tiles, device % tiles
        line = (group // 2 * tiles + tile) * here // LANES
        k = (line // part + group) % 2
        got = got_ref[device * part : (device + 2) * part, :]
        sums[k] = got if sums[k] is None else sums[k] + got
    one, two = [x[:part] + x[part:] for x in sums]
    coarse = jnp.concatenate(
        [jnp.where(parity == 0, one, two), jnp.where(parity == 0, two, one)], axis=0
    )

    def first_lane(m):
        line = (m // per_group * 2 + parity) * per_group + m % per_group
        return pl.multiple_of(line * LANES, LANES)

    inner = products(coarse, mine_ref, here, first_lane)
    other = products(coarse, theirs_ref, here, first_lane)
    for m in range(lines):
        place = slice(m * LANES, (m + 1) * LANES)
        term = mine_ref[:here, place] * inner + theirs_ref[:here, place] * other
        value_ref[m : m + 1, :] = jnp.sum(term, axis=0, keepdims=True)
    value = value_ref[...]
    slots_ref[pl.ds(0, lines, stride=4), :] = interleave(value, term_ref[0])
    slots_ref[pl.ds(1, lines, stride=4), :] = ring_ref[0]
    slots_ref[pl.ds(2, lines, stride=4), :] = interleave(shift(value, LANES // 2, 1), term_ref[1])
    slots_ref[pl.ds(3, lines, stride=4), :] = ring_ref[1]


def prolong_line(line, first, shape):
    index = jnp.broadcast_to(first + lane_iota(shape) // FAC, shape)
    return gather_lanes(jnp.broadcast_to(line, shape), index)


def last_kernel(grid, got_ref, rhs_ref, diag_ref, weight_ref, smooth_ref, out_ref):
    rows, cols = out_ref.shape
    block_rows, per_row, per_tile = rows // FAC, cols // FAC, LANES // FAC
    here = block_rows * per_row
    shape = (SUB, LANES)
    lane = lane_iota(shape)
    g = lax.axis_index("grp")
    in_side = lane_inside(grid, lane)
    total = got_ref[:SUB, :]
    for at in range(SUB, got_ref.shape[0], SUB):
        total = total + got_ref[at : at + SUB, :]
    total = total + shift(total, SUB // 2, 0)
    total = total + shift(total, SUB // 4, 0)
    second, ring = total[:1], total[1:2]

    def pick(line, at):
        return gather_lanes(jnp.broadcast_to(line, shape), jnp.full(shape, at, jnp.int32))

    def band(line, at, side, step):
        parts = [prolong_line(line, at + q * per_tile, shape) for q in range(cols // LANES)]
        beside, other = pick(ring, side + per_row - 1 - step), pick(ring, side + step)
        return parts + [jnp.where(in_side, jnp.where(lane < LANES // 2, beside, other), 0.0)]

    bands = [band(second, here + a * per_row, here + a * per_row, 0) for a in range(block_rows)]
    under = [jnp.where(g < grid[0] - 1, x, 0.0) for x in band(ring, per_row, here + per_row, 1)]
    over = [jnp.where(g > 0, x, 0.0) for x in band(ring, 0, here, 1)]
    tiles = [bands[at // FAC] for at in range(0, rows, SUB)] + [under, over]
    field = jnp.concatenate(
        [jnp.concatenate([tile[q] for tile in tiles], axis=0) for q in range(len(over))], axis=1
    )
    field = smooth_ref[...] + MIX * field
    rhs = rhs_ref[...]
    weight = weight_ref[...]
    rest = rhs - (6.0 + diag_ref[...]) * field + neighbour_sum(field)
    smooth = weight * rest
    for _ in range(SWEEPS - 1):
        smooth = (1.0 - OMEGA) * smooth + weight * (rest + neighbour_sum(smooth))
    base = field[:rows, :cols] + smooth[:rows, :cols]
    line = MIX * second
    for a in range(rows // FAC):
        for q in range(cols // LANES):
            part = prolong_line(line, a * per_row + q * (LANES // FAC), (SUB, LANES))
            for low in range(a * FAC, (a + 1) * FAC, SUB):
                where = (slice(low, low + SUB), slice(q * LANES, (q + 1) * LANES))
                out_ref[where] = base[where] + part


def shards(right_side, diagonal, inverse_factor):
    groups, tiles = lax.axis_size("grp"), lax.axis_size("tile")
    grid = (groups, tiles)
    count = groups * tiles
    rows, cols = right_side.shape
    points = inverse_factor.shape[1]
    high = points // LANES
    assert 2 * inverse_factor.shape[0] == LANES and rows == 2 * FAC and groups % 2 == 0
    everyone = ("grp", "tile")

    def exchange(slots):
        lines = slots.shape[0] // count
        got = lax.all_to_all(slots.reshape(count, lines * LANES), everyone, 0, 0, tiled=True)
        return got.reshape(count * lines, LANES)

    width = 2 * rows * HALO // LANES + 1
    here = inverse_factor.shape[0]
    shapes = [(count * width, LANES), (rows, cols), (rows, cols), (here + HALO, points)]
    shapes += [(HALO, 2 * cols)] if groups > 2 else []
    slots, right_side, diagonal, mine, *edges = pl.pallas_call(
        functools.partial(start_kernel, grid),
        out_shape=[jax.ShapeDtypeStruct(s, jnp.float32) for s in shapes],
        in_specs=[pl.BlockSpec(memory_space=pltpu.HBM)] * 3,
        out_specs=[VMEM] * len(shapes),
        scratch_shapes=[pltpu.SemaphoreType.DMA((3,))],
        compiler_params=pltpu.CompilerParams(vmem_limit_bytes=limit(points)),
    )(
        *[
            pltpu.with_memory_space_constraint(x, pltpu.HBM)
            for x in (right_side, diagonal, inverse_factor)
        ]
    )
    theirs = lax.ppermute(mine, "grp", [(i, i ^ 1) for i in range(groups)])
    far = []
    if groups > 2:
        across = [(i, i + 1) for i in range(1, groups - 1, 2)]
        across += [(j, i) for i, j in across]
        far = [lax.ppermute(edges[0], "grp", across)]
    got = exchange(slots)

    wide = (rows + 2 * HALO, cols + LANES)
    rhs, diag, weight, smooth, term, ring, slots = call(
        points,
        functools.partial(middle_kernel, grid, width),
        [wide] * 4 + [(2, high, LANES)] * 2 + [(count * high // 4, LANES)],
        5 + len(far),
        [(high, LANES)],
    )(got, right_side, diagonal, mine, theirs, *far)
    got = exchange(slots)

    (slots,) = call(
        points,
        functools.partial(second_kernel, grid, high // groups),
        [(2 * count, LANES)],
        5,
        [(high, LANES)],
    )(got, mine, theirs, term, ring)
    got = exchange(slots)
    (field,) = call(
        points, functools.partial(last_kernel, grid), [(rows, cols)], 5
    )(got, rhs, diag, weight, smooth)
    return field


def solution(mesh):
    placed = (P("grp", "tile"), P("grp", "tile"), P(("grp", "tile"), None))

    return jax.shard_map(
        shards, mesh=mesh, in_specs=placed, out_specs=P("grp", "tile"), check_vma=False
    )
```
